256 devices in a mesh: dom: 64 (over z, y, core), rep: 4 (over x).
Axes of the slice: x: 4, y: 4, z: 8, core: 2. Of those that a mesh axis runs over, the one named last changes fastest.
Arguments:
- node_features: bfloat16 [262144, 128], P(('rep', 'dom')), parts along dimension 0, may hold values from -6 to 6
- edge_features: bfloat16 [688128, 128], P(('rep', 'dom')), parts along dimension 0, may hold values from -6 to 6
- node_cotangent: bfloat16 [262144, 128], P(('rep', 'dom')), parts along dimension 0, may hold values from -6 to 6
- edge_cotangent: bfloat16 [688128, 128], P(('rep', 'dom')), parts along dimension 0, may hold values from -6 to 6
- edge_in_weight: bfloat16 [384, 128], replicated, may hold values from -0.3125 to 0.3125
- edge_in_bias: float32 [128], replicated, may hold values from -3 to 3
- edge_out_weight: bfloat16 [128, 128], replicated, may hold values from -0.5 to 0.5
- edge_out_bias: float32 [128], replicated, may hold values from -3 to 3
- node_in_weight: bfloat16 [256, 128], replicated, may hold values from -0.375 to 0.375
- node_in_bias: float32 [128], replicated, may hold values from -3 to 3
- node_out_weight: bfloat16 [128, 128], replicated, may hold values from -0.5 to 0.5
- edge_ends: int32 [2, 1344], replicated, may hold values from 0 to 511, as said below
- live_elements: int32 [256], P(('rep', 'dom')), parts along dimension 0, may hold values from 1 to 2, as said below
- shared_nodes: int32 [256, 4, 128], P(('rep', 'dom')), parts along dimension 0, may hold values from 0 to 1023, as said below
- shared_counts: int32 [256, 4], P(('rep', 'dom')), parts along dimension 0, may hold values from 32 to 128, as said below
- multiplicity: int32 [262144], P(('rep', 'dom')), parts along dimension 0, may hold values from 1 to 515
Outputs:
- node_gradient: bfloat16 [262144, 128], P(('rep', 'dom')), parts along dimension 0
- edge_gradient: bfloat16 [688128, 128], P(('rep', 'dom')), parts along dimension 0
- edge_in_weight_gradient: float32 [1536, 128], P('rep'), parts along dimension 0
- edge_in_bias_gradient: float32 [512], P('rep'), parts along dimension 0
- edge_out_weight_gradient: float32 [512, 128], P('rep'), parts along dimension 0
- edge_out_bias_gradient: float32 [512], P('rep'), parts along dimension 0
- node_in_weight_gradient: float32 [1024, 128], P('rep'), parts along dimension 0
- node_in_bias_gradient: float32 [512], P('rep'), parts along dimension 0
- node_out_weight_gradient: float32 [512, 128], P('rep'), parts along dimension 0
- node_out_bias_gradient: float32 [512], P('rep'), parts along dimension 0
The draws below stay inside these ranges and needn't reach their ends.
There are 4 independent parts, one for each index of `rep`. The reference program is written for one: setup_inputs(seed, part) draws one part's arguments, and reference() takes and returns one part's arrays. A program takes and returns all parts, laid end to end along the dimension named above; an argument that names none is the same for every part. Nothing has to cross between parts.
Inputs may be any that keep to these rules, and one draw needn't show every extreme that they name: `edge_ends`: each edge joins two nodes next to each other on the element's 8 x 8 x 8 lattice of nodes. `live_elements`: some partition has all 2 slots live. `shared_nodes`: entry s of a partition's list for neighbour k is the node paired with entry s of that neighbour's list for neighbour k xor 1; entries below the count name nodes of live slots; entries at or beyond it are 0. `shared_counts`: both lists of a pair have the same count; some pair has 128 entries.
All inputs are finite; a program needn't handle non-finite values.
Results may differ from the reference program's by a relative error of at most 0.0056.
Values sent between devices are 32-bit elements; how exact they have to be, the bound alone decides.
No kernel may reach another device: no remote copies, remote signals or barrier semaphores. Data moves between devices by JAX's collectives and lax.ppermute only.
A program may use at most 64 MiB of HBM per device.

```python
import math
import jax
import jax.numpy as jnp
from jax import lax

D = 128
HID = 128
NPE = 512
EPE = 1344
S_MAX = 128
E_DEV = 2
NODES = 65536
EDGES = 172032
N_DOM = 64


def draw_layout(key):
    subkeys = [jax.random.fold_in(key, 7001 + number) for number in range(8)]
    device = jnp.arange(N_DOM, dtype=jnp.int32)
    raw_draw = jax.random.randint(subkeys[0], (N_DOM,), 0, E_DEV + 1, dtype=jnp.int32)
    element_counts = jnp.minimum(1 + raw_draw * raw_draw // E_DEV, E_DEV)
    busiest = jax.random.randint(subkeys[1], (), 0, N_DOM, dtype=jnp.int32)
    element_counts = jnp.where(device == busiest, E_DEV, element_counts).astype(jnp.int32)
    quarter = N_DOM // 4
    pair_lengths = jax.random.randint(subkeys[2], (2 * N_DOM,), max(S_MAX // 4, 1), S_MAX + 1, dtype=jnp.int32)
    full_pair = jax.random.randint(subkeys[3], (), 0, 2 * N_DOM, dtype=jnp.int32)
    pair_lengths = jnp.where(jnp.arange(2 * N_DOM, dtype=jnp.int32) == full_pair, S_MAX, pair_lengths).reshape(2, N_DOM)
    hop_sizes = jnp.array([1, quarter], dtype=jnp.int32)
    upper_device = (device[None, :] + hop_sizes[:, None]) % N_DOM
    lower_device = (device[None, :] - hop_sizes[:, None]) % N_DOM
    entry_index = jnp.arange(S_MAX, dtype=jnp.int32)[None, None, :]
    low_side = jax.random.randint(subkeys[4], (2, N_DOM, S_MAX), 0, element_counts[None, :, None] * NPE, dtype=jnp.int32)
    high_side = jax.random.randint(subkeys[5], (2, N_DOM, S_MAX), 0, element_counts[upper_device][:, :, None] * NPE, dtype=jnp.int32)
    entry_used = entry_index < pair_lengths[:, :, None]
    low_side = jnp.where(entry_used, low_side, 0)
    high_side = jnp.where(entry_used, high_side, 0)
    kinds = jnp.arange(2, dtype=jnp.int32)[:, None]
    from_high = high_side[kinds, lower_device]
    node_lists = jnp.stack([low_side[0], from_high[0], low_side[1], from_high[1]], axis=1).astype(jnp.int32)
    high_lengths = pair_lengths[kinds, lower_device]
    list_lengths = jnp.stack([pair_lengths[0], high_lengths[0], pair_lengths[1], high_lengths[1]], axis=1).astype(jnp.int32)
    listed = (entry_index < list_lengths[:, :, None]).astype(jnp.int32).reshape(-1)
    rows = (device[:, None, None] * (E_DEV * NPE) + node_lists).reshape(-1)
    appearances = jnp.zeros((N_DOM * E_DEV * NPE,), jnp.int32).at[rows].add(listed)
    extra_copies = jax.random.randint(subkeys[6], (N_DOM * E_DEV * NPE,), 0, 3, dtype=jnp.int32)
    copies = jnp.minimum(1 + appearances + extra_copies, 4 * S_MAX + 3)
    crowded = jax.random.randint(subkeys[7], (), 0, N_DOM * E_DEV * NPE, dtype=jnp.int32)
    copies = jnp.where(jnp.arange(N_DOM * E_DEV * NPE, dtype=jnp.int32) == crowded, 4 * S_MAX + 3, copies).astype(jnp.int32)
    return (element_counts, node_lists, list_lengths, copies)


def draw_live_elements(key, part):
    return draw_layout(key)[0]


def draw_shared_nodes(key, part):
    return draw_layout(key)[1]


def draw_shared_counts(key, part):
    return draw_layout(key)[2]


def draw_multiplicity(key, part):
    return draw_layout(key)[3]


def draw_edge_ends(key, part):
    start_node = jax.random.randint(jax.random.fold_in(key, 9101), (EPE,), 0, NPE, dtype=jnp.int32)
    direction = jax.random.randint(jax.random.fold_in(key, 9102), (EPE,), 0, 3, dtype=jnp.int32)
    step_sign = 2 * jax.random.randint(jax.random.fold_in(key, 9103), (EPE,), 0, 2, dtype=jnp.int32) - 1
    stride = jnp.where(direction == 0, 64, jnp.where(direction == 1, 8, 1)).astype(jnp.int32)
    coordinate = start_node // stride % 8
    outside = (coordinate + step_sign < 0) | (coordinate + step_sign > 7)
    step_sign = jnp.where(outside, -step_sign, step_sign)
    return jnp.stack([start_node, start_node + step_sign * stride]).astype(jnp.int32)


def steps_of(stream_key, dims, split, low, top_value):
    def one(dim, parts):
        draws = jax.random.uniform(jax.random.fold_in(jax.random.fold_in(stream_key, 6), dim), (parts,), jnp.float32, low / len(split), top_value / len(split))
        return jnp.repeat(jnp.exp(draws), dims[dim] // parts).reshape((-1,) + (1,) * (len(dims) - dim - 1))

    factor_of = one(*split[0])
    for cut in split[1:]:
        factor_of = factor_of * one(*cut)
    return factor_of


def bell_draw(rng, extent, width, reach, pieces=(), held_as=jnp.bfloat16):
    entries = width * jax.random.normal(rng, extent, jnp.float32)
    if pieces:
        entries = entries * steps_of(rng, extent, pieces, -0.22, 0.18)
    return jnp.clip(entries, -reach, reach).astype(held_as)


def setup_inputs(seed: int = 0, part: int = 0) -> dict:
    key_list = jax.random.split(jax.random.key(seed), 17)
    part_splits = jax.random.split(jax.random.fold_in(key_list[16], part), 17)
    return {
        "node_features": bell_draw(part_splits[0], (NODES, D), 1.0, 6.0, ((0, 64),)),
        "edge_features": bell_draw(part_splits[1], (EDGES, D), 1.0, 6.0, ((0, 64),)),
        "node_cotangent": bell_draw(part_splits[2], (NODES, D), 1.0, 6.0, ((0, 64),)),
        "edge_cotangent": bell_draw(part_splits[3], (EDGES, D), 1.0, 6.0, ((0, 64),)),
        "edge_in_weight": bell_draw(key_list[4], (3 * D, HID), (3 * D) ** -0.5, 0.3125),
        "edge_in_bias": bell_draw(key_list[5], (HID,), 0.5, 3.0, (), jnp.float32),
        "edge_out_weight": bell_draw(key_list[6], (HID, D), HID ** -0.5, 0.5),
        "edge_out_bias": bell_draw(key_list[7], (D,), 0.5, 3.0, (), jnp.float32),
        "node_in_weight": bell_draw(key_list[8], (2 * D, HID), (2 * D) ** -0.5, 0.375),
        "node_in_bias": bell_draw(key_list[9], (HID,), 0.5, 3.0, (), jnp.float32),
        "node_out_weight": bell_draw(key_list[10], (HID, D), HID ** -0.5, 0.5),
        "edge_ends": draw_edge_ends(jax.random.fold_in(key_list[16], 71), part),
        "live_elements": draw_live_elements(jax.random.fold_in(jax.random.fold_in(key_list[16], part), 71), part),
        "shared_nodes": draw_shared_nodes(jax.random.fold_in(jax.random.fold_in(key_list[16], part), 71), part),
        "shared_counts": draw_shared_counts(jax.random.fold_in(jax.random.fold_in(key_list[16], part), 71), part),
        "multiplicity": draw_multiplicity(jax.random.fold_in(jax.random.fold_in(key_list[16], part), 71), part),
    }


def silu_slope(linear):
    squashed = jax.nn.sigmoid(linear)
    return squashed * (1.0 + linear * (1.0 - squashed))

def contract_rows(left, right):
    return lax.dot_general(left, right, (((0,), (0,)), ((), ())), preferred_element_type=jnp.float32)

def edge_forward(blocks, edge_rows, edge_ends, edge_in_weight, edge_in_bias, edge_out_weight, edge_out_bias):
    feature_width = blocks.shape[2]
    source = jnp.take(blocks, edge_ends[0], axis=1).reshape(-1, feature_width)
    target = jnp.take(blocks, edge_ends[1], axis=1).reshape(-1, feature_width)
    joined = jnp.concatenate([source, target, edge_rows], axis=1)
    edge_linear = jnp.dot(joined, edge_in_weight, preferred_element_type=jnp.float32) + edge_in_bias
    edge_hidden = jax.nn.silu(edge_linear).astype(jnp.bfloat16)
    new_edges = edge_rows.astype(jnp.float32) + jnp.dot(edge_hidden, edge_out_weight, preferred_element_type=jnp.float32) + edge_out_bias
    return (joined, edge_linear, edge_hidden, new_edges)

def collect(new_edges, edge_ends, slot_count, element_nodes):
    feature_width = new_edges.shape[1]
    grouped = new_edges.reshape(slot_count, -1, feature_width)
    return jnp.zeros((slot_count, element_nodes, feature_width), jnp.float32).at[:, edge_ends[1]].add(grouped)

def edge_backward(joined, edge_linear, edge_hidden, edge_cot, edge_ends, edge_in_weight, edge_out_weight, slot_count, element_nodes):
    feature_width = edge_cot.shape[1]
    cot_half = edge_cot.astype(jnp.bfloat16)
    out_weight_term = contract_rows(edge_hidden, cot_half)
    out_bias_term = lax.optimization_barrier(jnp.sum(cot_half.astype(jnp.float32), axis=0))
    hidden_back = jnp.dot(cot_half, edge_out_weight.T, preferred_element_type=jnp.float32)
    edge_back = (hidden_back * silu_slope(edge_linear)).astype(jnp.bfloat16)
    in_weight_term = contract_rows(joined, edge_back)
    in_bias_term = lax.optimization_barrier(jnp.sum(edge_back.astype(jnp.float32), axis=0))
    joined_back = jnp.dot(edge_back, edge_in_weight.T, preferred_element_type=jnp.float32)
    from_source = joined_back[:, :feature_width].reshape(slot_count, -1, feature_width)
    from_target = joined_back[:, feature_width:2 * feature_width].reshape(slot_count, -1, feature_width)
    block_back = jnp.zeros((slot_count, element_nodes, feature_width), jnp.float32)
    block_back = block_back.at[:, edge_ends[0]].add(from_source).at[:, edge_ends[1]].add(from_target)
    edge_result = (edge_cot + joined_back[:, 2 * feature_width:]).astype(jnp.bfloat16)
    return (block_back, edge_result, (in_weight_term, in_bias_term, out_weight_term, out_bias_term))

def reference(node_features, edge_features, node_cotangent, edge_cotangent, edge_in_weight, edge_in_bias, edge_out_weight, edge_out_bias, node_in_weight, node_in_bias, node_out_weight, edge_ends, live_elements, shared_nodes, shared_counts, multiplicity):
    device_nodes = E_DEV * NPE
    device_edges = E_DEV * EPE
    live_slots = jnp.arange(E_DEV, dtype=jnp.int32)[None, :] < live_elements[:, None]
    node_live = jnp.repeat(live_slots, NPE, axis=1).reshape(-1)
    edge_live = jnp.repeat(live_slots, EPE, axis=1).reshape(-1)
    node_cot = jnp.where(node_live[:, None], node_cotangent, jnp.zeros_like(node_cotangent))
    edge_given = jnp.where(edge_live[:, None], edge_cotangent.astype(jnp.float32), jnp.zeros((1, D), jnp.float32))
    node_blocks = node_features.reshape(N_DOM, E_DEV, NPE, D)
    edge_blocks = edge_features.reshape(N_DOM, device_edges, D)

    def forward_device(bundle):
        outputs = edge_forward(bundle[0], bundle[1], edge_ends, edge_in_weight, edge_in_bias, edge_out_weight, edge_out_bias)
        return collect(outputs[3], edge_ends, E_DEV, NPE)
    aggregate = lax.map(forward_device, (node_blocks, edge_blocks)).reshape(NODES, D)
    quarter = N_DOM // 4
    offsets = jnp.array([1, -1, quarter, -quarter], dtype=jnp.int32)
    device = jnp.arange(N_DOM, dtype=jnp.int32)[:, None, None]
    neighbour = jnp.arange(4, dtype=jnp.int32)[None, :, None]
    entry_index = jnp.arange(S_MAX, dtype=jnp.int32)[None, None, :]
    partner_device = (device + offsets[neighbour]) % N_DOM
    own_rows = (device * device_nodes + shared_nodes).reshape(-1).astype(jnp.int32)
    partner_rows = (partner_device * device_nodes + shared_nodes[partner_device, neighbour ^ 1, entry_index]).reshape(-1).astype(jnp.int32)
    entry_valid = (entry_index < shared_counts[:, :, None]).reshape(-1)

    def partner_sum(values):
        moved = jnp.where(entry_valid[:, None], values[partner_rows], jnp.zeros((1, D), jnp.float32))
        return values + jnp.zeros_like(values).at[own_rows].add(moved)
    copies = multiplicity[:, None].astype(jnp.float32)
    consistent = partner_sum(aggregate) / copies
    node_input = jnp.concatenate([node_features, consistent.astype(jnp.bfloat16)], axis=1)
    node_linear = jnp.dot(node_input, node_in_weight, preferred_element_type=jnp.float32) + node_in_bias
    node_hidden = jax.nn.silu(node_linear).astype(jnp.bfloat16)
    node_out_term = contract_rows(node_hidden, node_cot)
    node_out_bias_term = lax.optimization_barrier(jnp.sum(node_cot.astype(jnp.float32), axis=0))
    hidden_back = jnp.dot(node_cot, node_out_weight.T, preferred_element_type=jnp.float32)
    node_back = (hidden_back * silu_slope(node_linear)).astype(jnp.bfloat16)
    node_in_term = contract_rows(node_input, node_back)
    node_in_bias_term = lax.optimization_barrier(jnp.sum(node_back.astype(jnp.float32), axis=0))
    node_input_back = jnp.dot(node_back, node_in_weight.T, preferred_element_type=jnp.float32)
    consistent_back = node_input_back[:, D:] / copies
    aggregate_back = partner_sum(consistent_back)
    gathered_back = jnp.take(aggregate_back.reshape(N_DOM * E_DEV, NPE, D), edge_ends[1], axis=1).reshape(EDGES, D)
    edge_cot = edge_given + gathered_back

    def backward_device(bundle):
        joined, edge_linear, edge_hidden, unused = edge_forward(bundle[0], bundle[1], edge_ends, edge_in_weight, edge_in_bias, edge_out_weight, edge_out_bias)
        return edge_backward(joined, edge_linear, edge_hidden, bundle[2], edge_ends, edge_in_weight, edge_out_weight, E_DEV, NPE)
    block_back, edge_result, edge_terms = lax.map(backward_device, (node_blocks, edge_blocks, edge_cot.reshape(N_DOM, device_edges, D)))
    edge_scale = 1.0 / math.sqrt(EDGES)
    node_scale = 1.0 / math.sqrt(NODES)
    node_result = (node_cot.astype(jnp.float32) + node_input_back[:, :D] + block_back.reshape(NODES, D)).astype(jnp.bfloat16)
    return (node_result, edge_result.reshape(EDGES, D), lax.optimization_barrier(jnp.sum(edge_terms[0], axis=0)) * edge_scale, lax.optimization_barrier(jnp.sum(edge_terms[1], axis=0)) * edge_scale, lax.optimization_barrier(jnp.sum(edge_terms[2], axis=0)) * edge_scale, lax.optimization_barrier(jnp.sum(edge_terms[3], axis=0)) * edge_scale, node_in_term * node_scale, node_in_bias_term * node_scale, node_out_term * node_scale, node_out_bias_term * node_scale)
```

```python
import math

import jax
import jax.numpy as jnp
from jax import lax
from jax.experimental import pallas as pl
from jax.experimental.pallas import tpu as pltpu
from jax.sharding import Mesh, PartitionSpec as P

NPE = 512
LANES = 128
BLOCK = 256
F32 = jnp.float32
BF16 = jnp.bfloat16
AXES = ("z", "y", "c")
VMEM = pl.BlockSpec(memory_space=pltpu.VMEM)
SMEM = pl.BlockSpec(memory_space=pltpu.SMEM)


def padded(count):
    return -(-count // LANES) * LANES


def dot(left, right):
    return jnp.dot(left, right, preferred_element_type=F32)


def dot_t(left, right):
    return lax.dot_general(left, right, (((1,), (1,)), ((), ())), preferred_element_type=F32)


def dot_rows(left, right):
    return lax.dot_general(left, right, (((0,), (0,)), ((), ())), preferred_element_type=F32)


def split(value):
    high = value.astype(BF16)
    low = (value - high.astype(F32)).astype(BF16)
    return high, low


def as_column(row):
    return jnp.transpose(jnp.broadcast_to(row, (LANES, LANES)))


def hot(flags):
    return jnp.where(flags, 1.0, 0.0).astype(BF16)


def pick_table(row, width):
    column = as_column(row)
    lane = lax.broadcasted_iota(jnp.int32, (LANES, LANES), 1)
    tiles = [hot(column == lane + start) for start in range(0, width, LANES)]
    return jnp.concatenate(tiles, axis=1)


def spread_table(row, height):
    return hot(lax.broadcasted_iota(jnp.int32, (height, row.shape[1]), 0) == row)


def list_rows(lists_ref, counts_ref):
    core = lax.axis_index("c")
    odd = lax.rem(lax.div(lax.axis_index("z"), 2), 2)
    lane = lax.broadcasted_iota(jnp.int32, (1, LANES), 1)
    rows = [jnp.where(lane < counts_ref[0, k], lists_ref[k : k + 1, :], -1) for k in range(4)]

    def ordered(flag, first, second):
        chosen = jnp.full((1, LANES), flag, jnp.int32) == 0
        return jnp.where(chosen, first, second), jnp.where(chosen, second, first)

    return ordered(core, rows[0], rows[1]) + ordered(odd, rows[2], rows[3])


def outgoing(rows, values, refs):
    table = jnp.concatenate([pick_table(row, values.shape[0]) for row in rows], axis=0)
    both = dot(table, jnp.concatenate(split(values), axis=1))
    for k, ref in enumerate(refs):
        part = both[k * LANES : (k + 1) * LANES]
        ref[...] = part[:, :LANES] + part[:, LANES:]


def incoming(rows, refs, height):
    table = jnp.concatenate([spread_table(row, height) for row in rows], axis=1)
    arrived = jnp.concatenate([ref[...] for ref in refs], axis=0)
    both = dot(table, jnp.concatenate(split(arrived), axis=1))
    return both[:, :LANES] + both[:, LANES:]


def blocks_of(count):
    return [(start, min(BLOCK, count - start)) for start in range(0, count, BLOCK)]


def stage_ends(ends_ref, ends_sc):
    ends_sc[...] = jnp.full(ends_sc.shape, -1, jnp.int32)
    ends_sc[0:2, 0 : ends_ref.shape[1]] = ends_ref[...]


def edge_rows_table(ends_sc, side, start, size):
    parts = [
        pick_table(ends_sc[side : side + 1, first : first + LANES], NPE)
        for first in range(start, start + size, LANES)
    ]
    return jnp.concatenate(parts, axis=0)[:size]


def forward_kernel(
    counts_ref, ends_ref, lists_ref, nf_ref, ef_ref, wi_ref, bi_ref, wo_ref, bo_ref,
    agg_ref, out0, out1, out2, out3, hid_ref, slope_ref,
    ends_sc, rows_sc, spread_sc,
):
    edges = ends_ref.shape[1]
    width = padded(edges)
    stage_ends(ends_ref, ends_sc)
    nf = nf_ref[...]
    from_source = dot(nf, wi_ref[0:128, :]).astype(BF16)
    from_target = dot(nf, wi_ref[128:256, :]).astype(BF16)
    table_rows = jnp.concatenate(
        [
            jnp.concatenate([from_source[:NPE], from_source[NPE:]], axis=1),
            jnp.concatenate([from_target[:NPE], from_target[NPE:]], axis=1),
        ],
        axis=0,
    )
    for start, size in blocks_of(edges):
        table = jnp.concatenate(
            [
                edge_rows_table(ends_sc, 0, start, size),
                edge_rows_table(ends_sc, 1, start, size),
            ],
            axis=1,
        )
        ends_part = dot(table, table_rows)
        for slot in range(2):
            first = slot * edges + start
            own = ef_ref[first : first + size, :]
            linear = (
                ends_part[:, slot * LANES : (slot + 1) * LANES]
                + dot(own, wi_ref[256:384, :])
                + bi_ref[...]
            )
            squashed = jax.nn.sigmoid(linear)
            hidden = (linear * squashed).astype(BF16)
            hid_ref[first : first + size, :] = hidden
            slope_ref[first : first + size, :] = squashed * (1.0 + linear * (1.0 - squashed))
            rows_sc[start : start + size, slot * LANES : (slot + 1) * LANES] = own
            rows_sc[start : start + size, (2 + slot) * LANES : (3 + slot) * LANES] = hidden
    rows_sc[edges:width, :] = jnp.zeros((width - edges, 4 * LANES), BF16)
    degree = jnp.zeros((NPE, LANES), F32)
    for first in range(0, width, LANES):
        table = spread_table(ends_sc[1:2, first : first + LANES], NPE)
        spread_sc[:, first : first + LANES] = table
        degree = degree + table.astype(F32)
    degree = jnp.sum(degree, axis=1, keepdims=True)
    sums = dot(spread_sc[...], rows_sc[...])
    for slot in range(2):
        high, low = split(sums[:, (2 + slot) * LANES : (3 + slot) * LANES])
        agg_ref[slot * NPE : (slot + 1) * NPE, :] = (
            sums[:, slot * LANES : (slot + 1) * LANES]
            + (dot(high, wo_ref[...]) + dot(low, wo_ref[...]))
            + degree * bo_ref[...]
        )
    outgoing(list_rows(lists_ref, counts_ref), agg_ref[...], (out0, out1, out2, out3))


def node_kernel(
    counts_ref, live_ref, lists_ref, agg_ref, in0, in1, in2, in3, mult_ref,
    nf_ref, nc_ref, wn_ref, bn_ref, wo_ref,
    back_ref, out0, out1, out2, out3, part_ref, terms_ref,
):
    nodes = nf_ref.shape[0]
    rows = list_rows(lists_ref, counts_ref)
    copies = jnp.concatenate(
        [as_column(mult_ref[b : b + 1, :].astype(F32)) for b in range(nodes // LANES)], axis=0
    )
    total = agg_ref[...] + incoming(rows, (in0, in1, in2, in3), nodes)
    consistent = (total / copies).astype(BF16)
    node_input = jnp.concatenate([nf_ref[...], consistent], axis=1)
    linear = dot(node_input, wn_ref[...]) + bn_ref[...]
    squashed = jax.nn.sigmoid(linear)
    hidden = (linear * squashed).astype(BF16)
    live = lax.broadcasted_iota(jnp.int32, (nodes, LANES), 0) < NPE * live_ref[0]
    cot = jnp.where(live, nc_ref[...].astype(F32), 0.0)
    cot_half = cot.astype(BF16)
    slope = squashed * (1.0 + linear * (1.0 - squashed))
    back = (dot_t(cot_half, wo_ref[...]) * slope).astype(BF16)
    consistent_back = dot_t(back, wn_ref[128:256, :]) / copies
    back_ref[...] = consistent_back
    outgoing(rows, consistent_back, (out0, out1, out2, out3))
    part_ref[...] = cot + dot_t(back, wn_ref[0:128, :])
    terms_ref[0:256, :] = dot_rows(node_input, back)
    terms_ref[256:384, :] = dot_rows(hidden, cot_half)
    terms_ref[384:386, :] = jnp.zeros((2, LANES), F32)
    terms_ref[386:387, :] = jnp.sum(back.astype(F32), axis=0, keepdims=True)
    terms_ref[387:388, :] = jnp.sum(cot, axis=0, keepdims=True)
    terms_ref[388:512, :] = jnp.zeros((124, LANES), F32)


def backward_kernel(
    counts_ref, live_ref, ends_ref, lists_ref, back_ref, in0, in1, in2, in3,
    ec_ref, hid_ref, slope_ref, ef_ref, nf_ref, part_ref, terms_ref, wi_ref, wo_ref,
    node_ref, edge_ref, mine_ref, theirs_ref,
    ends_sc, rows_sc, spread_sc, half_sc, eback_sc, sums_sc,
):
    edges = ends_ref.shape[1]
    width = padded(edges)
    nodes = nf_ref.shape[0]
    stage_ends(ends_ref, ends_sc)
    rows = list_rows(lists_ref, counts_ref)
    agg_back = (back_ref[...] + incoming(rows, (in0, in1, in2, in3), nodes)).astype(BF16)
    table_rows = jnp.concatenate([agg_back[:NPE], agg_back[NPE:]], axis=1)
    in_bias = jnp.zeros((1, LANES), F32)
    out_bias = jnp.zeros((1, LANES), F32)
    for start, size in blocks_of(edges):
        gathered = dot(edge_rows_table(ends_sc, 1, start, size), table_rows)
        for slot in range(2):
            first = slot * edges + start
            given = ec_ref[first : first + size, :].astype(F32)
            given = jnp.where(
                jnp.full((size, LANES), live_ref[0], jnp.int32) > slot, given, 0.0
            )
            cot = given + gathered[:, slot * LANES : (slot + 1) * LANES]
            half = cot.astype(BF16)
            back = (
                dot_t(half, wo_ref[...]) * slope_ref[first : first + size, :]
            ).astype(BF16)
            edge_ref[first : first + size, :] = (
                cot + dot_t(back, wi_ref[256:384, :])
            ).astype(BF16)
            half_sc[first : first + size, :] = half
            eback_sc[first : first + size, :] = back
            rows_sc[start : start + size, slot * LANES : (slot + 1) * LANES] = back
            in_bias = in_bias + jnp.sum(back.astype(F32), axis=0, keepdims=True)
            out_bias = out_bias + jnp.sum(half.astype(F32), axis=0, keepdims=True)
    rows_sc[edges:width, :] = jnp.zeros((width - edges, 2 * LANES), BF16)
    for first in range(0, width, LANES):
        for side in range(2):
            spread_sc[side * NPE : (side + 1) * NPE, first : first + LANES] = spread_table(
                ends_sc[side : side + 1, first : first + LANES], NPE
            )
    sums = dot(spread_sc[...], rows_sc[...])
    by_source = jnp.concatenate([sums[:NPE, :LANES], sums[:NPE, LANES:]], axis=0)
    by_target = jnp.concatenate([sums[NPE:, :LANES], sums[NPE:, LANES:]], axis=0)
    source_high, source_low = split(by_source)
    target_high, target_low = split(by_target)
    node_ref[...] = (
        part_ref[...]
        + (dot_t(source_high, wi_ref[0:128, :]) + dot_t(source_low, wi_ref[0:128, :]))
        + (dot_t(target_high, wi_ref[128:256, :]) + dot_t(target_low, wi_ref[128:256, :]))
    ).astype(BF16)
    pieces = dot_rows(
        nf_ref[...],
        jnp.concatenate([source_high, target_high, source_low, target_low], axis=1),
    )
    sums_sc[0:128, :] = pieces[:, 0:128] + pieces[:, 256:384]
    sums_sc[128:256, :] = pieces[:, 128:256] + pieces[:, 384:512]
    sums_sc[256:384, :] = dot_rows(ef_ref[...], eback_sc[...])
    sums_sc[384:512, :] = dot_rows(hid_ref[...], half_sc[...])
    sums_sc[512:1024, :] = terms_ref[...]
    sums_sc[896:897, :] = in_bias
    sums_sc[897:898, :] = out_bias
    first_core = jnp.full((512, LANES), lax.axis_index("c"), jnp.int32) == 0
    edge_half = sums_sc[0:512, :]
    node_half = sums_sc[512:1024, :]
    mine_ref[...] = jnp.where(first_core, edge_half, node_half)
    theirs_ref[...] = jnp.where(first_core, node_half, edge_half)


def finish_kernel(edge_scale, node_scale, own_ref, other_ref, ei, eib, eo, eob, ni, nib, no, nob):
    first_core = jnp.full((512, LANES), lax.axis_index("c"), jnp.int32) == 0
    own = own_ref[...]
    other = other_ref[...]
    edge_half = jnp.where(first_core, own, other)
    node_half = jnp.where(first_core, other, own)
    ei[...] = edge_half[0:384] * edge_scale
    eo[...] = edge_half[384:512] * edge_scale
    ni[...] = node_half[0:256] * node_scale
    no[...] = node_half[256:384] * node_scale
    eib[...] = node_half[384:385] * edge_scale
    eob[...] = node_half[385:386] * edge_scale
    nib[...] = node_half[386:387] * node_scale
    nob[...] = node_half[387:388] * node_scale


def call(kernel, out_shapes, specs, scratch, args, flops, moved):
    return pl.pallas_call(
        kernel,
        out_shape=[jax.ShapeDtypeStruct(shape, dtype) for shape, dtype in out_shapes],
        in_specs=specs,
        out_specs=[VMEM] * len(out_shapes),
        scratch_shapes=scratch,
        compiler_params=pltpu.CompilerParams(vmem_limit_bytes=40 * 1024 * 1024),
        cost_estimate=pl.CostEstimate(flops=flops, bytes_accessed=moved, transcendentals=0),
    )(*args)


def exchanged(messages):
    def near(device):
        return device ^ 1

    def next_chip(device):
        return device + 1 if device % 2 else device - 1

    count = lax.axis_size(AXES)
    quarter = count // 4

    def far_up(device):
        return device + quarter if (device // quarter) % 2 == 0 else device - quarter

    def far_down(device):
        return device - quarter if (device // quarter) % 2 == 0 else device + quarter

    return [
        lax.ppermute(message, AXES, [(s, swap(s) % count) for s in range(count)])
        for message, swap in zip(messages, (near, next_chip, far_up, far_down))
    ]


def body(
    node_features,
    edge_features,
    node_cotangent,
    edge_cotangent,
    edge_in_weight,
    edge_in_bias,
    edge_out_weight,
    edge_out_bias,
    node_in_weight,
    node_in_bias,
    node_out_weight,
    edge_ends,
    live_elements,
    shared_nodes,
    shared_counts,
    multiplicity,
):
    nodes, width = node_features.shape
    edges = edge_features.shape[0]
    devices = lax.axis_size(AXES)
    element_edges = edge_ends.shape[1]
    lists = shared_nodes.reshape(shared_nodes.shape[1:])
    copies = multiplicity.reshape(nodes // LANES, LANES)
    message = ((LANES, width), F32)
    ends_scratch = pltpu.VMEM((8, padded(element_edges)), jnp.int32)
    rows_height = padded(element_edges)

    aggregate, *messages, edge_hidden, edge_slope = call(
        forward_kernel,
        [((nodes, width), F32)] + [message] * 4 + [((edges, width), BF16), ((edges, width), F32)],
        [SMEM] + [VMEM] * 8,
        [
            ends_scratch,
            pltpu.VMEM((rows_height, 4 * LANES), BF16),
            pltpu.VMEM((NPE, rows_height), BF16),
        ],
        (
            shared_counts,
            edge_ends,
            lists,
            node_features,
            edge_features,
            edge_in_weight,
            edge_in_bias.reshape(1, -1),
            edge_out_weight,
            edge_out_bias.reshape(1, -1),
        ),
        2_000_000_000,
        4_000_000,
    )
    arrived = exchanged(messages)
    consistent_back, *messages, node_part, node_terms = call(
        node_kernel,
        [((nodes, width), F32)] + [message] * 4 + [((nodes, width), F32), ((512, width), F32)],
        [SMEM, SMEM] + [VMEM] * 12,
        [],
        (
            shared_counts,
            live_elements,
            lists,
            aggregate,
            *arrived,
            copies,
            node_features,
            node_cotangent,
            node_in_weight,
            node_in_bias.reshape(1, -1),
            node_out_weight,
        ),
        800_000_000,
        2_000_000,
    )
    arrived = exchanged(messages)
    node_result, edge_result, mine, theirs = call(
        backward_kernel,
        [
            ((nodes, width), BF16),
            ((edges, width), BF16),
            ((512, width), F32),
            ((512, width), F32),
        ],
        [SMEM, SMEM] + [VMEM] * 16,
        [
            ends_scratch,
            pltpu.VMEM((rows_height, 2 * LANES), BF16),
            pltpu.VMEM((2 * NPE, rows_height), BF16),
            pltpu.VMEM((edges, LANES), BF16),
            pltpu.VMEM((edges, LANES), BF16),
            pltpu.VMEM((1024, LANES), F32),
        ],
        (
            shared_counts,
            live_elements,
            edge_ends,
            lists,
            consistent_back,
            *arrived,
            edge_cotangent,
            edge_hidden,
            edge_slope,
            edge_features,
            node_features,
            node_part,
            node_terms,
            edge_in_weight,
            edge_out_weight,
        ),
        2_000_000_000,
        6_000_000,
    )
    other_core = [(0, 1), (1, 0)]
    chips = devices // 2
    half = mine + lax.ppermute(theirs, "c", other_core)
    half = half.reshape(chips, 512 // chips, width)
    share = lax.all_to_all(half, ("z", "y"), 0, 0, tiled=True).sum(axis=0)
    own = lax.all_to_all(
        jnp.broadcast_to(share, (chips, *share.shape)), ("z", "y"), 0, 0, tiled=True
    ).reshape(512, width)
    other = lax.ppermute(own, "c", other_core)
    edge_scale = 1.0 / math.sqrt(edges * devices)
    node_scale = 1.0 / math.sqrt(nodes * devices)

    def finish(*refs):
        finish_kernel(edge_scale, node_scale, *refs)

    ei, eib, eo, eob, ni, nib, no, nob = call(
        finish,
        [
            ((384, width), F32),
            ((1, width), F32),
            ((128, width), F32),
            ((1, width), F32),
            ((256, width), F32),
            ((1, width), F32),
            ((128, width), F32),
            ((1, width), F32),
        ],
        [VMEM] * 2,
        [],
        (own, other),
        1_000_000,
        1_000_000,
    )
    return (
        node_result,
        edge_result,
        ei,
        eib.reshape(-1),
        eo,
        eob.reshape(-1),
        ni,
        nib.reshape(-1),
        no,
        nob.reshape(-1),
    )


def solution(mesh):
    grid = mesh.devices.reshape(8, 4, 2, 4)
    mesh = Mesh(grid, ("z", "y", "c", "rep"))
    rows = ("rep", "z", "y", "c")
    in_specs = (
        P(rows, None),
        P(rows, None),
        P(rows, None),
        P(rows, None),
        P(),
        P(),
        P(),
        P(),
        P(),
        P(),
        P(),
        P(),
        P(rows),
        P(rows, None, None),
        P(rows, None),
        P(rows),
    )
    out_specs = (
        P(rows, None),
        P(rows, None),
        P("rep", None),
        P("rep"),
        P("rep", None),
        P("rep"),
        P("rep", None),
        P("rep"),
        P("rep", None),
        P("rep"),
    )
    return jax.shard_map(body, mesh=mesh, in_specs=in_specs, out_specs=out_specs, check_vma=False)
```

```python
import math

import jax
import jax.numpy as jnp
from jax import lax
from jax.experimental import pallas as pl
from jax.experimental.pallas import tpu as pltpu
from jax.sharding import Mesh, PartitionSpec as P

NPE = 512
LANES = 128
BLOCK = 256
F32 = jnp.float32
BF16 = jnp.bfloat16
AXES = ("z", "y", "c")
VMEM = pl.BlockSpec(memory_space=pltpu.VMEM)
SMEM = pl.BlockSpec(memory_space=pltpu.SMEM)
HBM = pl.BlockSpec(memory_space=pltpu.HBM)


def padded(count):
    return -(-count // LANES) * LANES


def dot(left, right):
    return jnp.dot(left, right, preferred_element_type=F32)


def dot_t(left, right):
    return lax.dot_general(left, right, (((1,), (1,)), ((), ())), preferred_element_type=F32)


def dot_rows(left, right):
    return lax.dot_general(left, right, (((0,), (0,)), ((), ())), preferred_element_type=F32)


def split(value):
    high = value.astype(BF16)
    low = (value - high.astype(F32)).astype(BF16)
    return high, low


def as_column(row):
    return jnp.transpose(jnp.broadcast_to(row, (LANES, LANES)))


def hot(flags):
    return jnp.where(flags, 1.0, 0.0).astype(BF16)


def pick_table(row, width):
    column = as_column(row)
    lane = lax.broadcasted_iota(jnp.int32, (LANES, LANES), 1)
    tiles = [hot(column == lane + start) for start in range(0, width, LANES)]
    return jnp.concatenate(tiles, axis=1)


def spread_table(row, height):
    return hot(lax.broadcasted_iota(jnp.int32, (height, row.shape[1]), 0) == row)


def list_rows(lists_ref, counts_ref):
    core = lax.axis_index("c")
    odd = lax.rem(lax.div(lax.axis_index("z"), 2), 2)
    lane = lax.broadcasted_iota(jnp.int32, (1, LANES), 1)
    rows = [jnp.where(lane < counts_ref[0, k], lists_ref[k : k + 1, :], -1) for k in range(4)]

    def ordered(flag, first, second):
        chosen = jnp.full((1, LANES), flag, jnp.int32) == 0
        return jnp.where(chosen, first, second), jnp.where(chosen, second, first)

    near, next_chip = ordered(core, rows[0], rows[1])
    return ordered(odd, rows[2], rows[3]) + (next_chip, near)


def outgoing(table_ref, values, refs):
    both = dot(table_ref[...], jnp.concatenate(split(values), axis=1))
    for k, ref in enumerate(refs):
        part = both[k * LANES : (k + 1) * LANES]
        ref[...] = part[:, :LANES] + part[:, LANES:]


def incoming(table_ref, refs):
    arrived = jnp.concatenate([ref[...] for ref in refs], axis=0)
    both = dot(table_ref[...], jnp.concatenate(split(arrived), axis=1))
    return both[:, :LANES] + both[:, LANES:]


def blocks_of(count):
    return [(start, min(BLOCK, count - start)) for start in range(0, count, BLOCK)]


def stage_ends(ends_ref, ends_sc):
    ends_sc[...] = jnp.full(ends_sc.shape, -1, jnp.int32)
    ends_sc[0:2, 0 : ends_ref.shape[1]] = ends_ref[...]


def edge_rows_table(ends_sc, side, start, size):
    parts = [
        pick_table(ends_sc[side : side + 1, first : first + LANES], NPE)
        for first in range(start, start + size, LANES)
    ]
    return jnp.concatenate(parts, axis=0)[:size]


def forward_kernel(
    counts_hbm, ends_hbm, lists_hbm, nf_hbm, ef_hbm, wi_hbm, bi_hbm, wo_hbm, bo_hbm,
    agg_ref, out0, out1, out2, out3, hid_ref, slope_ref, table_ref, spread_ref, pick_ref,
    counts_ref, ends_ref, lists_ref, nf_ref, ef_ref, wi_ref, bi_ref, wo_ref, bo_ref,
    sems, ends_sc, rows_sc,
):
    pairs = (
        (ends_hbm, ends_ref),
        (nf_hbm, nf_ref),
        (wi_hbm, wi_ref),
        (ef_hbm, ef_ref),
        (bi_hbm, bi_ref),
        (wo_hbm, wo_ref),
        (bo_hbm, bo_ref),
        (lists_hbm, lists_ref),
        (counts_hbm, counts_ref),
    )
    loads = [
        pltpu.make_async_copy(source, target, sems.at[k])
        for k, (source, target) in enumerate(pairs)
    ]
    for load in loads:
        load.start()
    edges = ends_ref.shape[1]
    width = padded(edges)
    loads[0].wait()
    stage_ends(ends_ref, ends_sc)
    degree = jnp.zeros((NPE, LANES), F32)
    for first in range(0, width, LANES):
        table = spread_table(ends_sc[1:2, first : first + LANES], NPE)
        spread_ref[:, first : first + LANES] = table
        degree = degree + table.astype(F32)
    degree = jnp.sum(degree, axis=1, keepdims=True)
    loads[1].wait()
    loads[2].wait()
    nf = nf_ref[...]
    from_source = dot(nf, wi_ref[0:128, :]).astype(BF16)
    from_target = dot(nf, wi_ref[128:256, :]).astype(BF16)
    table_rows = jnp.concatenate(
        [
            jnp.concatenate([from_source[:NPE], from_source[NPE:]], axis=1),
            jnp.concatenate([from_target[:NPE], from_target[NPE:]], axis=1),
        ],
        axis=0,
    )
    for load in loads[3:]:
        load.wait()
    for start, size in blocks_of(edges):
        by_target = edge_rows_table(ends_sc, 1, start, size)
        table_ref[start : start + size, :] = by_target
        table = jnp.concatenate([edge_rows_table(ends_sc, 0, start, size), by_target], axis=1)
        ends_part = dot(table, table_rows)
        for slot in range(2):
            first = slot * edges + start
            own = ef_ref[first : first + size, :]
            linear = (
                ends_part[:, slot * LANES : (slot + 1) * LANES]
                + dot(own, wi_ref[256:384, :])
                + bi_ref[...]
            )
            squashed = jax.nn.sigmoid(linear)
            hidden = (linear * squashed).astype(BF16)
            hid_ref[first : first + size, :] = hidden
            slope_ref[first : first + size, :] = squashed * (1.0 + linear * (1.0 - squashed))
            rows_sc[start : start + size, slot * LANES : (slot + 1) * LANES] = own
            rows_sc[start : start + size, (2 + slot) * LANES : (3 + slot) * LANES] = hidden
    rows_sc[edges:width, :] = jnp.zeros((width - edges, 4 * LANES), BF16)
    sums = dot(spread_ref[...], rows_sc[...])
    for slot in range(2):
        high, low = split(sums[:, (2 + slot) * LANES : (3 + slot) * LANES])
        agg_ref[slot * NPE : (slot + 1) * NPE, :] = (
            sums[:, slot * LANES : (slot + 1) * LANES]
            + (dot(high, wo_ref[...]) + dot(low, wo_ref[...]))
            + degree * bo_ref[...]
        )
    values = agg_ref[...]
    for k, row in enumerate(list_rows(lists_ref, counts_ref)):
        pick_ref[k * LANES : (k + 1) * LANES, :] = pick_table(row, values.shape[0])
    outgoing(pick_ref, values, (out0, out1, out2, out3))


def prepare_kernel(
    counts_ref, live_ref, ends_ref, lists_ref, mult_ref, nf_ref, nc_ref, wn_ref, bn_ref, wo_ref,
    spread_ref, arrive_ref, linear_ref, hback_ref, cot_ref, copies_ref,
    ends_sc,
):
    nodes = nf_ref.shape[0]
    stage_ends(ends_ref, ends_sc)
    for first in range(0, ends_sc.shape[1], LANES):
        spread_ref[:, first : first + LANES] = spread_table(
            ends_sc[0:1, first : first + LANES], NPE
        )
    for k, row in enumerate(list_rows(lists_ref, counts_ref)):
        arrive_ref[:, k * LANES : (k + 1) * LANES] = spread_table(row, nodes)
    live = lax.broadcasted_iota(jnp.int32, (nodes, LANES), 0) < NPE * live_ref[0]
    cot = jnp.where(live, nc_ref[...].astype(F32), 0.0).astype(BF16)
    cot_ref[...] = cot
    linear_ref[...] = dot(nf_ref[...], wn_ref[0:128, :]) + bn_ref[...]
    hback_ref[...] = dot_t(cot, wo_ref[...])
    for b in range(nodes // LANES):
        copies_ref[b * LANES : (b + 1) * LANES, :] = as_column(mult_ref[b : b + 1, :].astype(F32))


def node_kernel(
    agg_ref, in0, in1, in2, in3, arrive_ref, pick_ref, linear_ref, hback_ref, copies_ref, wn_ref,
    cback_ref, out0, out1, out2, out3, cons_ref, hid_ref, back_ref,
):
    copies = copies_ref[...]
    total = agg_ref[...] + incoming(arrive_ref, (in0, in1, in2, in3))
    consistent = (total / copies).astype(BF16)
    linear = linear_ref[...] + dot(consistent, wn_ref[128:256, :])
    squashed = jax.nn.sigmoid(linear)
    slope = squashed * (1.0 + linear * (1.0 - squashed))
    back = (hback_ref[...] * slope).astype(BF16)
    consistent_back = dot_t(back, wn_ref[128:256, :]) / copies
    cback_ref[...] = consistent_back
    outgoing(pick_ref, consistent_back, (out0, out1, out2, out3))
    cons_ref[...] = consistent
    hid_ref[...] = (linear * squashed).astype(BF16)
    back_ref[...] = back


def node_sums_kernel(
    nf_ref, cons_ref, hid_ref, back_ref, cot_ref, wn_ref,
    part_ref, terms_ref,
):
    back = back_ref[...]
    cot_half = cot_ref[...]
    cot = cot_half.astype(F32)
    part_ref[...] = cot + dot_t(back, wn_ref[0:128, :])
    terms_ref[0:128, :] = dot_rows(nf_ref[...], back)
    terms_ref[128:256, :] = dot_rows(cons_ref[...], back)
    terms_ref[256:384, :] = dot_rows(hid_ref[...], cot_half)
    terms_ref[384:386, :] = jnp.zeros((2, LANES), F32)
    terms_ref[386:387, :] = jnp.sum(back.astype(F32), axis=0, keepdims=True)
    terms_ref[387:388, :] = jnp.sum(cot, axis=0, keepdims=True)
    terms_ref[388:512, :] = jnp.zeros((124, LANES), F32)


def backward_kernel(
    live_ref, cback_ref, in0, in1, in2, in3, arrive_ref, table_ref, spread_s_ref, spread_t_ref,
    ec_ref, hid_ref, slope_ref, ef_ref, nf_ref, terms_ref, wo_ref,
    cot_ref, eback_ref, sums_ref, mine_ref, theirs_ref,
    rows_sc, half_sc, terms_sc,
):
    edges = table_ref.shape[0]
    width = padded(edges)
    agg_back = (cback_ref[...] + incoming(arrive_ref, (in0, in1, in2, in3))).astype(BF16)
    table_rows = jnp.concatenate([agg_back[:NPE], agg_back[NPE:]], axis=1)
    in_bias = jnp.zeros((1, LANES), F32)
    out_bias = jnp.zeros((1, LANES), F32)
    for start, size in blocks_of(edges):
        gathered = dot(table_ref[start : start + size, :], table_rows)
        for slot in range(2):
            first = slot * edges + start
            given = ec_ref[first : first + size, :].astype(F32)
            given = jnp.where(
                jnp.full((size, LANES), live_ref[0], jnp.int32) > slot, given, 0.0
            )
            cot = given + gathered[:, slot * LANES : (slot + 1) * LANES]
            half = cot.astype(BF16)
            back = (
                dot_t(half, wo_ref[...]) * slope_ref[first : first + size, :]
            ).astype(BF16)
            cot_ref[first : first + size, :] = cot
            half_sc[first : first + size, :] = half
            eback_ref[first : first + size, :] = back
            rows_sc[start : start + size, slot * LANES : (slot + 1) * LANES] = back
            in_bias = in_bias + jnp.sum(back.astype(F32), axis=0, keepdims=True)
            out_bias = out_bias + jnp.sum(half.astype(F32), axis=0, keepdims=True)
    rows_sc[edges:width, :] = jnp.zeros((width - edges, 2 * LANES), BF16)
    by_source = dot(spread_s_ref[...], rows_sc[...])
    by_target = dot(spread_t_ref[...], rows_sc[...])
    sums_ref[0:NPE, 0:LANES] = by_source[:, :LANES]
    sums_ref[NPE : 2 * NPE, 0:LANES] = by_source[:, LANES:]
    sums_ref[0:NPE, LANES:] = by_target[:, :LANES]
    sums_ref[NPE : 2 * NPE, LANES:] = by_target[:, LANES:]
    both = dot_rows(nf_ref[...], jnp.concatenate(split(sums_ref[...]), axis=1))
    terms_sc[0:128, :] = both[:, 0:128] + both[:, 256:384]
    terms_sc[128:256, :] = both[:, 128:256] + both[:, 384:512]
    terms_sc[256:384, :] = dot_rows(ef_ref[...], eback_ref[...])
    terms_sc[384:512, :] = dot_rows(hid_ref[...], half_sc[...])
    terms_sc[512:1024, :] = terms_ref[...]
    terms_sc[896:897, :] = in_bias
    terms_sc[897:898, :] = out_bias
    core = lax.axis_index("c")
    place = lax.axis_index("y")
    for k in range(4):
        block = lax.bitwise_xor(place, k) * LANES
        kept = pl.multiple_of(core * 512 + block, LANES)
        sent = pl.multiple_of((1 - core) * 512 + block, LANES)
        mine_ref[k * LANES : (k + 1) * LANES, :] = terms_sc[pl.ds(kept, LANES), :]
        theirs_ref[k * LANES : (k + 1) * LANES, :] = terms_sc[pl.ds(sent, LANES), :]


def results_kernel(cot_ref, eback_ref, sums_ref, part_ref, wi_ref, node_ref, edge_ref):
    high, low = split(sums_ref[...])
    node_ref[...] = (
        part_ref[...]
        + (dot_t(high[:, :LANES], wi_ref[0:128, :]) + dot_t(low[:, :LANES], wi_ref[0:128, :]))
        + (dot_t(high[:, LANES:], wi_ref[128:256, :]) + dot_t(low[:, LANES:], wi_ref[128:256, :]))
    ).astype(BF16)
    edge_ref[...] = (cot_ref[...] + dot_t(eback_ref[...], wi_ref[256:384, :])).astype(BF16)


def finish_kernel(
    edge_scale, node_scale, own_ref, other_ref, ei, eib, eo, eob, ni, nib, no, nob, sums_sc
):
    core = lax.axis_index("c")
    place = lax.axis_index("y")
    for k in range(4):
        block = lax.bitwise_xor(place, k) * LANES
        kept = pl.multiple_of(core * 512 + block, LANES)
        sent = pl.multiple_of((1 - core) * 512 + block, LANES)
        sums_sc[pl.ds(kept, LANES), :] = own_ref[k * LANES : (k + 1) * LANES, :]
        sums_sc[pl.ds(sent, LANES), :] = other_ref[k * LANES : (k + 1) * LANES, :]
    ei[...] = sums_sc[0:384, :] * edge_scale
    eo[...] = sums_sc[384:512, :] * edge_scale
    ni[...] = sums_sc[512:768, :] * node_scale
    no[...] = sums_sc[768:896, :] * node_scale
    eib[...] = sums_sc[896:897, :] * edge_scale
    eob[...] = sums_sc[897:898, :] * edge_scale
    nib[...] = sums_sc[898:899, :] * node_scale
    nob[...] = sums_sc[899:900, :] * node_scale


def call(kernel, out_shapes, specs, scratch, args, flops, moved):
    return pl.pallas_call(
        kernel,
        out_shape=[jax.ShapeDtypeStruct(shape, dtype) for shape, dtype in out_shapes],
        in_specs=specs,
        out_specs=[VMEM] * len(out_shapes),
        scratch_shapes=scratch,
        compiler_params=pltpu.CompilerParams(vmem_limit_bytes=40 * 1024 * 1024),
        cost_estimate=pl.CostEstimate(flops=flops, bytes_accessed=moved, transcendentals=0),
    )(*args)


def in_hbm(*values):
    return tuple(pltpu.with_memory_space_constraint(value, pltpu.HBM) for value in values)


def exchanged(messages):
    def near(device):
        return device ^ 1

    def next_chip(device):
        return device + 1 if device % 2 else device - 1

    count = lax.axis_size(AXES)
    quarter = count // 4

    def far_up(device):
        return device + quarter if (device // quarter) % 2 == 0 else device - quarter

    def far_down(device):
        return device - quarter if (device // quarter) % 2 == 0 else device + quarter

    def swapped(message, swap):
        return lax.ppermute(message, AXES, [(s, swap(s) % count) for s in range(count)])

    swaps = (far_up, far_down, next_chip, near)
    return [swapped(message, swap) for message, swap in zip(messages, swaps)]


def swapped_with(value, axis, partner):
    return lax.ppermute(value, axis, [(s, partner(s)) for s in range(lax.axis_size(axis))])


def summed_along_y(mine, theirs):
    half = mine + swapped_with(theirs, "c", lambda s: 1 - s)
    blocks = [half[k * LANES : (k + 1) * LANES] for k in range(4)]
    two = swapped_with(blocks[2], "y", lambda s: s ^ 2)
    three = swapped_with(blocks[3], "y", lambda s: s ^ 3)
    one = swapped_with(blocks[1], "y", lambda s: s ^ 1)
    return (blocks[0] + one) + (two + three)


def summed_along_z(total):
    three = swapped_with(total, "z", lambda s: s ^ 3)
    two = swapped_with(total, "z", lambda s: s ^ 2)
    one = swapped_with(total, "z", lambda s: s ^ 1)
    return (total + one) + (two + three)


def shared(total):
    two = swapped_with(total, "y", lambda s: s ^ 2)
    three = swapped_with(total, "y", lambda s: s ^ 3)
    one = swapped_with(total, "y", lambda s: s ^ 1)
    own = jnp.concatenate([total, one, two, three], axis=0)
    return own, swapped_with(own, "c", lambda s: 1 - s)


def body(
    node_features,
    edge_features,
    node_cotangent,
    edge_cotangent,
    edge_in_weight,
    edge_in_bias,
    edge_out_weight,
    edge_out_bias,
    node_in_weight,
    node_in_bias,
    node_out_weight,
    edge_ends,
    live_elements,
    shared_nodes,
    shared_counts,
    multiplicity,
):
    nodes, width = node_features.shape
    edges = edge_features.shape[0]
    devices = lax.axis_size(AXES)
    element_edges = edge_ends.shape[1]
    lists = shared_nodes.reshape(shared_nodes.shape[1:])
    copies = multiplicity.reshape(nodes // LANES, LANES)
    message = ((LANES, width), F32)
    node_f32 = ((nodes, width), F32)
    node_bf16 = ((nodes, width), BF16)
    edge_f32 = ((edges, width), F32)
    edge_bf16 = ((edges, width), BF16)
    rows_height = padded(element_edges)
    ends_scratch = pltpu.VMEM((8, rows_height), jnp.int32)
    listed = 4 * LANES

    forward_args = in_hbm(
        shared_counts,
        edge_ends,
        lists,
        node_features,
        edge_features,
        edge_in_weight,
        edge_in_bias.reshape(1, -1),
        edge_out_weight,
        edge_out_bias.reshape(1, -1),
    )
    aggregate, *messages, edge_hidden, edge_slope, table, spread_target, pick = call(
        forward_kernel,
        [node_f32]
        + [message] * 4
        + [
            edge_bf16,
            edge_f32,
            ((element_edges, NPE), BF16),
            ((NPE, rows_height), BF16),
            ((listed, nodes), BF16),
        ],
        [HBM] * 9,
        [pltpu.SMEM(shared_counts.shape, jnp.int32)]
        + [pltpu.VMEM(arg.shape, arg.dtype) for arg in forward_args[1:]]
        + [
            pltpu.SemaphoreType.DMA((9,)),
            ends_scratch,
            pltpu.VMEM((rows_height, 4 * LANES), BF16),
        ],
        forward_args,
        2_000_000_000,
        4_000_000,
    )
    arrived = exchanged(messages)
    spread_source, arrive, linear_part, hidden_back, node_cot, copies_wide = call(
        prepare_kernel,
        [
            ((NPE, rows_height), BF16),
            ((nodes, listed), BF16),
            node_f32,
            node_f32,
            node_bf16,
            node_f32,
        ],
        [SMEM, SMEM] + [VMEM] * 8,
        [ends_scratch],
        (
            shared_counts,
            live_elements,
            edge_ends,
            lists,
            copies,
            node_features,
            node_cotangent,
            node_in_weight,
            node_in_bias.reshape(1, -1),
            node_out_weight,
        ),
        1_000_000_000,
        4_000_000,
    )
    consistent_back, *messages, consistent, node_hidden, node_back = call(
        node_kernel,
        [node_f32] + [message] * 4 + [node_bf16] * 3,
        [VMEM] * 11,
        [],
        (
            aggregate,
            *arrived,
            arrive,
            pick,
            linear_part,
            hidden_back,
            copies_wide,
            node_in_weight,
        ),
        600_000_000,
        4_000_000,
    )
    arrived = exchanged(messages)
    node_part, node_terms = call(
        node_sums_kernel,
        [node_f32, ((512, width), F32)],
        [VMEM] * 6,
        [],
        (node_features, consistent, node_hidden, node_back, node_cot, node_in_weight),
        1_000_000_000,
        4_000_000,
    )
    edge_cot, edge_back, edge_sums, mine, theirs = call(
        backward_kernel,
        [
            edge_f32,
            edge_bf16,
            ((nodes, 2 * LANES), F32),
            ((512, width), F32),
            ((512, width), F32),
        ],
        [SMEM] + [VMEM] * 16,
        [
            pltpu.VMEM((rows_height, 2 * LANES), BF16),
            pltpu.VMEM((edges, LANES), BF16),
            pltpu.VMEM((1024, LANES), F32),
        ],
        (
            live_elements,
            consistent_back,
            *arrived,
            arrive,
            table,
            spread_source,
            spread_target,
            edge_cotangent,
            edge_hidden,
            edge_slope,
            edge_features,
            node_features,
            node_terms,
            edge_out_weight,
        ),
        2_000_000_000,
        6_000_000,
    )
    total = summed_along_y(mine, theirs)
    total = summed_along_z(total)
    total, edge_cot = lax.optimization_barrier((total, edge_cot))
    far = swapped_with(total, "z", lambda s: 7 - s)
    node_result, edge_result = call(
        results_kernel,
        [node_bf16, edge_bf16],
        [VMEM] * 5,
        [],
        (edge_cot, edge_back, edge_sums, node_part, edge_in_weight),
        2_000_000_000,
        6_000_000,
    )
    total, far, node_result = lax.optimization_barrier((total, far, node_result))
    own, other = shared(total + far)
    edge_scale = 1.0 / math.sqrt(edges * devices)
    node_scale = 1.0 / math.sqrt(nodes * devices)

    def finish(*refs):
        finish_kernel(edge_scale, node_scale, *refs)

    ei, eib, eo, eob, ni, nib, no, nob = call(
        finish,
        [
            ((384, width), F32),
            ((1, width), F32),
            ((128, width), F32),
            ((1, width), F32),
            ((256, width), F32),
            ((1, width), F32),
            ((128, width), F32),
            ((1, width), F32),
        ],
        [VMEM] * 2,
        [pltpu.VMEM((1024, LANES), F32)],
        (own, other),
        1_000_000,
        1_000_000,
    )
    return (
        node_result,
        edge_result,
        ei,
        eib.reshape(-1),
        eo,
        eob.reshape(-1),
        ni,
        nib.reshape(-1),
        no,
        nob.reshape(-1),
    )


def solution(mesh):
    grid = mesh.devices.reshape(8, 4, 2, 4)
    mesh = Mesh(grid, ("z", "y", "c", "rep"))
    rows = ("rep", "z", "y", "c")
    in_specs = (
        P(rows, None),
        P(rows, None),
        P(rows, None),
        P(rows, None),
        P(),
        P(),
        P(),
        P(),
        P(),
        P(),
        P(),
        P(),
        P(rows),
        P(rows, None, None),
        P(rows, None),
        P(rows),
    )
    out_specs = (
        P(rows, None),
        P(rows, None),
        P("rep", None),
        P("rep"),
        P("rep", None),
        P("rep"),
        P("rep", None),
        P("rep"),
        P("rep", None),
        P("rep"),
    )
    return jax.shard_map(body, mesh=mesh, in_specs=in_specs, out_specs=out_specs, check_vma=False)
```

```python
import math

import jax
import jax.numpy as jnp
from jax import lax
from jax.experimental import pallas as pl
from jax.experimental.pallas import tpu as pltpu
from jax.sharding import Mesh, PartitionSpec as P

NPE = 512
LANES = 128
BLOCK = 256
FORWARD_BLOCK = 1344
BACKWARD_BLOCK = 1344
QUARTER = 120
F32 = jnp.float32
BF16 = jnp.bfloat16
AXES = ("z", "y", "c")
VMEM = pl.BlockSpec(memory_space=pltpu.VMEM)
SMEM = pl.BlockSpec(memory_space=pltpu.SMEM)
HBM = pl.BlockSpec(memory_space=pltpu.HBM)


def padded(count):
    return -(-count // LANES) * LANES


def dot(left, right):
    return jnp.dot(left, right, preferred_element_type=F32)


def dot_t(left, right):
    return lax.dot_general(left, right, (((1,), (1,)), ((), ())), preferred_element_type=F32)


def dot_rows(left, right):
    return lax.dot_general(left, right, (((0,), (0,)), ((), ())), preferred_element_type=F32)


def split(value):
    high = value.astype(BF16)
    low = (value - high.astype(F32)).astype(BF16)
    return high, low


def as_column(row):
    return jnp.transpose(jnp.broadcast_to(row, (LANES, LANES)))


def hot(flags):
    return jnp.where(flags, jnp.ones(flags.shape, BF16), jnp.zeros(flags.shape, BF16))


def pick_table(row, width):
    column = as_column(row).astype(jnp.int16)
    lane = lax.broadcasted_iota(jnp.int32, (LANES, LANES), 1)
    tiles = [hot(column == (lane + start).astype(jnp.int16)) for start in range(0, width, LANES)]
    return jnp.concatenate(tiles, axis=1)


def spread_table(row, height):
    named = jnp.broadcast_to(row, (16, LANES)).astype(jnp.int16)
    named = jnp.concatenate([named] * (height // 16), axis=0)
    place = lax.broadcasted_iota(jnp.int32, (height, LANES), 0).astype(jnp.int16)
    return hot(place == named)


def list_rows(lists_ref, counts_ref):
    core = lax.axis_index("c")
    odd = lax.rem(lax.div(lax.axis_index("z"), 2), 2)
    lane = lax.broadcasted_iota(jnp.int32, (1, LANES), 1)
    rows = [jnp.where(lane < counts_ref[0, k], lists_ref[k : k + 1, :], -1) for k in range(4)]

    def ordered(flag, first, second):
        chosen = jnp.full((1, LANES), flag, jnp.int32) == 0
        return jnp.where(chosen, first, second), jnp.where(chosen, second, first)

    near, next_chip = ordered(core, rows[0], rows[1])
    up, down = ordered(odd, rows[2], rows[3])
    return (next_chip, up, down, near)


def outgoing(table_ref, values, refs):
    both = dot(table_ref[...], jnp.concatenate(split(values), axis=1))
    for k, ref in enumerate(refs):
        part = both[k * LANES : (k + 1) * LANES]
        ref[...] = part[:, :LANES] + part[:, LANES:]


def incoming(table_ref, refs):
    arrived = jnp.concatenate([ref[...] for ref in refs], axis=0)
    both = dot(table_ref[...], jnp.concatenate(split(arrived), axis=1))
    return both[:, :LANES] + both[:, LANES:]


def spans(count, block):
    return [(start, min(block, count - start)) for start in range(0, count, block)]


def blocks_of(count):
    return spans(count, BLOCK)


def twice(block):
    zero = jnp.zeros_like(block)
    return jnp.concatenate(
        [jnp.concatenate([block, zero], axis=1), jnp.concatenate([zero, block], axis=1)], axis=0
    )


def beside(ref, start, size, edges):
    return jnp.concatenate(
        [ref[start : start + size, :], ref[edges + start : edges + start + size, :]], axis=1
    )


def stage_ends(ends_ref, ends_sc):
    ends_sc[...] = jnp.full(ends_sc.shape, -1, jnp.int32)
    ends_sc[0:2, 0 : ends_ref.shape[1]] = ends_ref[...]


def edge_rows_table(ends_sc, side, start, size):
    parts = [
        pick_table(ends_sc[side : side + 1, first : first + LANES], NPE)
        for first in range(start, start + size, LANES)
    ]
    return jnp.concatenate(parts, axis=0)[:size]


def forward_kernel(
    counts_hbm, ends_hbm, lists_hbm, nf_hbm, ef_hbm, wi_hbm, bi_hbm, wo_hbm, bo_hbm,
    agg_ref, out0, out1, out2, out3, hid_ref, slope_ref, table_ref, spread_ref, pick_ref,
    counts_ref, ends_ref, lists_ref, nf_ref, ef_ref, wi_ref, bi_ref, wo_ref, bo_ref,
    sems, ends_sc, rows_sc, source_sc,
):
    pairs = (
        (ends_hbm, ends_ref),
        (nf_hbm, nf_ref),
        (wi_hbm, wi_ref),
        (ef_hbm, ef_ref),
        (bi_hbm, bi_ref),
        (wo_hbm, wo_ref),
        (bo_hbm, bo_ref),
        (lists_hbm, lists_ref),
        (counts_hbm, counts_ref),
    )
    loads = [
        pltpu.make_async_copy(source, target, sems.at[k])
        for k, (source, target) in enumerate(pairs)
    ]
    for load in loads:
        load.start()
    edges = ends_ref.shape[1]
    width = padded(edges)
    loads[0].wait()
    stage_ends(ends_ref, ends_sc)
    for first in range(0, width, LANES):
        spread_ref[:, first : first + LANES] = spread_table(
            ends_sc[1:2, first : first + LANES], NPE
        )
    for start, size in blocks_of(edges):
        source_sc[start : start + size, :] = edge_rows_table(ends_sc, 0, start, size)
        table_ref[start : start + size, :] = edge_rows_table(ends_sc, 1, start, size)
    rows_sc[edges:width, :] = jnp.zeros((width - edges, 2 * LANES), BF16)
    for load in loads[1:]:
        load.wait()
    values_rows = list_rows(lists_ref, counts_ref)
    for k, row in enumerate(values_rows):
        pick_ref[k * LANES : (k + 1) * LANES, :] = pick_table(row, nf_ref.shape[0])
    in_weights = jnp.concatenate([wi_ref[0:128, :], wi_ref[128:256, :]], axis=1)
    ends_rows = dot(nf_ref[...], in_weights).astype(BF16)
    source_rows = jnp.concatenate([ends_rows[:NPE, :LANES], ends_rows[NPE:, :LANES]], axis=1)
    target_rows = jnp.concatenate([ends_rows[:NPE, LANES:], ends_rows[NPE:, LANES:]], axis=1)
    own_weight = twice(wi_ref[256:384, :])
    out_weight = twice(wo_ref[...])
    in_bias = jnp.concatenate([bi_ref[...]] * 2, axis=1)
    out_bias = jnp.concatenate([bo_ref[...]] * 2, axis=1)
    for start, size in spans(edges, FORWARD_BLOCK):
        own = beside(ef_ref, start, size, edges)
        linear = (
            dot(source_sc[start : start + size, :], source_rows)
            + dot(table_ref[start : start + size, :], target_rows)
            + dot(own, own_weight)
            + in_bias
        )
        squashed = jax.nn.sigmoid(linear)
        hidden = (linear * squashed).astype(BF16)
        hid_ref[start : start + size, :] = hidden
        slope_ref[start : start + size, :] = squashed * (1.0 + linear * (1.0 - squashed))
        rows_sc[start : start + size, :] = (
            own.astype(F32) + dot(hidden, out_weight) + out_bias
        ).astype(BF16)
    sums = dot(spread_ref[...], rows_sc[...])
    agg_ref[0:NPE, :] = sums[:, :LANES]
    agg_ref[NPE:, :] = sums[:, LANES:]
    outgoing(pick_ref, agg_ref[...], (out0, out1, out2, out3))


def block_starts():
    core = lax.axis_index("c")
    place = lax.axis_index("y")
    starts = []
    for k in range(4):
        block = lax.bitwise_xor(place, k) * QUARTER
        kept = pl.multiple_of(core * (4 * QUARTER) + block, 8)
        sent = pl.multiple_of((1 - core) * (4 * QUARTER) + block, 8)
        starts.append((kept, sent))
    return starts


def prepare_kernel(
    counts_ref, live_ref, ends_ref, lists_ref, mult_ref, nf_ref, nc_ref, wn_ref, bn_ref, wo_ref,
    spread_ref, arrive_ref, linear_ref, hback_ref, cot_ref, copies_ref,
    ends_sc,
):
    nodes = nf_ref.shape[0]
    stage_ends(ends_ref, ends_sc)
    for first in range(0, ends_sc.shape[1], LANES):
        spread_ref[:, first : first + LANES] = spread_table(
            ends_sc[0:1, first : first + LANES], NPE
        )
    for k, row in enumerate(list_rows(lists_ref, counts_ref)):
        arrive_ref[:, k * LANES : (k + 1) * LANES] = spread_table(row, nodes)
    live = lax.broadcasted_iota(jnp.int32, (nodes, LANES), 0) < NPE * live_ref[0]
    cot = jnp.where(live, nc_ref[...].astype(F32), 0.0).astype(BF16)
    cot_ref[...] = cot
    linear_ref[...] = dot(nf_ref[...], wn_ref[0:128, :]) + bn_ref[...]
    hback_ref[...] = dot_t(cot, wo_ref[...])
    for b in range(nodes // LANES):
        copies_ref[b * LANES : (b + 1) * LANES, :] = as_column(mult_ref[b : b + 1, :].astype(F32))


def node_kernel(
    agg_ref, in0, in1, in2, in3, arrive_ref, pick_ref, linear_ref, hback_ref, copies_ref, wn_ref,
    cback_ref, out0, out1, out2, out3, cons_ref, hid_ref, back_ref,
):
    copies = copies_ref[...]
    total = agg_ref[...] + incoming(arrive_ref, (in0, in1, in2, in3))
    consistent = (total / copies).astype(BF16)
    linear = linear_ref[...] + dot(consistent, wn_ref[128:256, :])
    squashed = jax.nn.sigmoid(linear)
    slope = squashed * (1.0 + linear * (1.0 - squashed))
    back = (hback_ref[...] * slope).astype(BF16)
    consistent_back = dot_t(back, wn_ref[128:256, :]) / copies
    cback_ref[...] = consistent_back
    outgoing(pick_ref, consistent_back, (out0, out1, out2, out3))
    cons_ref[...] = consistent
    hid_ref[...] = (linear * squashed).astype(BF16)
    back_ref[...] = back


def side_kernel(
    live_ref, nf_ref, cons_ref, hid_ref, back_ref, cot_ref, wn_ref, ef_ref, ec_ref, ehid_ref,
    spread_ref, wo_ref, part_ref, terms_ref, given_ref, eft_ref, nft_ref, hsumt_ref, outw_ref, wot_ref,
):
    back = back_ref[...]
    cot_half = cot_ref[...]
    cot = cot_half.astype(F32)
    part_ref[...] = cot + dot_t(back, wn_ref[0:128, :])
    terms_ref[0:128, :] = dot_rows(nf_ref[...], back)
    terms_ref[128:256, :] = dot_rows(cons_ref[...], back)
    terms_ref[256:384, :] = dot_rows(hid_ref[...], cot_half)
    terms_ref[384:448, :] = jnp.zeros((64, LANES), F32)
    terms_ref[386:387, :] = jnp.sum(back.astype(F32), axis=0, keepdims=True)
    terms_ref[387:388, :] = jnp.sum(cot, axis=0, keepdims=True)
    edges = ef_ref.shape[0] // 2
    live = jnp.full((edges, LANES), live_ref[0], jnp.int32)
    width = eft_ref.shape[1]
    for slot in range(2):
        rows = slice(slot * edges, (slot + 1) * edges)
        lanes = slice(slot * LANES, (slot + 1) * LANES)
        given_ref[:, lanes] = jnp.where(live > slot, ec_ref[rows, :].astype(F32), 0.0).astype(BF16)
        eft_ref[lanes, 0:edges] = jnp.transpose(ef_ref[rows, :].astype(F32)).astype(BF16)
    eft_ref[:, edges:] = jnp.zeros((2 * LANES, width - edges), BF16)
    nft_ref[...] = jnp.transpose(nf_ref[...].astype(F32)).astype(BF16)
    hidden = ehid_ref[...]
    filler = jnp.zeros((width - edges, 2 * LANES), BF16)
    sums = dot(spread_ref[...], jnp.concatenate([hidden, filler], axis=0))
    for slot in range(2):
        lanes = slice(slot * LANES, (slot + 1) * LANES)
        high, low = split(jnp.transpose(sums[:, lanes]))
        hsumt_ref[0:LANES, slot * NPE : (slot + 1) * NPE] = high
        hsumt_ref[LANES:, slot * NPE : (slot + 1) * NPE] = low
    both = dot_rows(hidden, given_ref[...])
    outw_ref[...] = both[:LANES, :LANES] + both[LANES:, LANES:]
    wot_ref[...] = twice(jnp.transpose(wo_ref[...].astype(F32)).astype(BF16))


def backward_kernel(
    cback_ref, in0, in1, in2, in3, arrive_ref, table_ref, spread_s_ref, spread_t_ref,
    given_ref, slope_ref, eft_ref, nft_ref, hsumt_ref, outw_ref, terms_ref, wot_ref,
    cot_ref, eback_ref, sums_ref, mine_ref, theirs_ref,
    terms_sc,
):
    edges = table_ref.shape[0]
    width = padded(edges)
    agg_back = (cback_ref[...] + incoming(arrive_ref, (in0, in1, in2, in3))).astype(BF16)
    table_rows = jnp.concatenate([agg_back[:NPE], agg_back[NPE:]], axis=1)
    in_bias = jnp.zeros((1, 2 * LANES), F32)
    out_bias = jnp.zeros((1, 2 * LANES), F32)
    for start, size in spans(edges, BACKWARD_BLOCK):
        rows = slice(start, start + size)
        cot = given_ref[rows, :].astype(F32) + dot(table_ref[rows, :], table_rows)
        half = cot.astype(BF16)
        back = (dot(half, wot_ref[...]) * slope_ref[rows, :]).astype(BF16)
        cot_ref[rows, :] = cot
        eback_ref[rows, :] = back
        in_bias = in_bias + jnp.sum(back.astype(F32), axis=0, keepdims=True)
        out_bias = out_bias + jnp.sum(half.astype(F32), axis=0, keepdims=True)
    eback_ref[edges:width, :] = jnp.zeros((width - edges, 2 * LANES), BF16)
    by_source = dot(spread_s_ref[...], eback_ref[...])
    by_target = dot(spread_t_ref[...], eback_ref[...])
    by_edge = dot(eft_ref[...], eback_ref[...])
    sums_ref[0:NPE, 0:LANES] = by_source[:, :LANES]
    sums_ref[NPE : 2 * NPE, 0:LANES] = by_source[:, LANES:]
    sums_ref[0:NPE, LANES:] = by_target[:, :LANES]
    sums_ref[NPE : 2 * NPE, LANES:] = by_target[:, LANES:]
    both = dot(nft_ref[...], jnp.concatenate(split(sums_ref[...]), axis=1))
    terms_sc[0:128, :] = both[:, 0:128] + both[:, 256:384]
    terms_sc[128:256, :] = both[:, 128:256] + both[:, 384:512]
    terms_sc[256:384, :] = by_edge[:LANES, :LANES] + by_edge[LANES:, LANES:]
    shared_part = dot(hsumt_ref[...], agg_back)
    terms_sc[384:512, :] = outw_ref[...] + (shared_part[:LANES] + shared_part[LANES:])
    terms_sc[512:960, :] = terms_ref[...]
    terms_sc[896:897, :] = in_bias[:, :LANES] + in_bias[:, LANES:]
    terms_sc[897:898, :] = out_bias[:, :LANES] + out_bias[:, LANES:]
    for k, (kept, sent) in enumerate(block_starts()):
        mine_ref[k * QUARTER : (k + 1) * QUARTER, :] = terms_sc[pl.ds(kept, QUARTER), :]
        theirs_ref[k * QUARTER : (k + 1) * QUARTER, :] = terms_sc[pl.ds(sent, QUARTER), :]


def results_kernel(cot_ref, eback_ref, sums_ref, part_ref, wi_ref, node_ref, edge_ref):
    high, low = split(sums_ref[...])
    node_ref[...] = (
        part_ref[...]
        + (dot_t(high[:, :LANES], wi_ref[0:128, :]) + dot_t(low[:, :LANES], wi_ref[0:128, :]))
        + (dot_t(high[:, LANES:], wi_ref[128:256, :]) + dot_t(low[:, LANES:], wi_ref[128:256, :]))
    ).astype(BF16)
    edges = cot_ref.shape[0]
    own_weight = twice(jnp.transpose(wi_ref[256:384, :].astype(F32)).astype(BF16))
    result = (cot_ref[...] + dot(eback_ref[0:edges, :], own_weight)).astype(BF16)
    edge_ref[0:edges, :] = result[:, :LANES]
    edge_ref[edges:, :] = result[:, LANES:]


def finish_kernel(
    edge_scale, node_scale, own_ref, other_ref, ei, eib, eo, eob, ni, nib, no, nob, sums_sc
):
    for k, (kept, sent) in enumerate(block_starts()):
        sums_sc[pl.ds(kept, QUARTER), :] = own_ref[k * QUARTER : (k + 1) * QUARTER, :]
        sums_sc[pl.ds(sent, QUARTER), :] = other_ref[k * QUARTER : (k + 1) * QUARTER, :]
    ei[...] = sums_sc[0:384, :] * edge_scale
    eo[...] = sums_sc[384:512, :] * edge_scale
    ni[...] = sums_sc[512:768, :] * node_scale
    no[...] = sums_sc[768:896, :] * node_scale
    eib[...] = sums_sc[896:897, :] * edge_scale
    eob[...] = sums_sc[897:898, :] * edge_scale
    nib[...] = sums_sc[898:899, :] * node_scale
    nob[...] = sums_sc[899:900, :] * node_scale


def call(kernel, out_shapes, specs, scratch, args, flops, moved):
    return pl.pallas_call(
        kernel,
        out_shape=[jax.ShapeDtypeStruct(shape, dtype) for shape, dtype in out_shapes],
        in_specs=specs,
        out_specs=[VMEM] * len(out_shapes),
        scratch_shapes=scratch,
        compiler_params=pltpu.CompilerParams(vmem_limit_bytes=40 * 1024 * 1024),
        cost_estimate=pl.CostEstimate(flops=flops, bytes_accessed=moved, transcendentals=0),
    )(*args)


def in_hbm(*values):
    return tuple(pltpu.with_memory_space_constraint(value, pltpu.HBM) for value in values)


def exchanged(messages):
    def near(device):
        return device ^ 1

    def next_chip(device):
        return device + 1 if device % 2 else device - 1

    count = lax.axis_size(AXES)
    quarter = count // 4

    def far_up(device):
        return device + quarter if (device // quarter) % 2 == 0 else device - quarter

    def far_down(device):
        return device - quarter if (device // quarter) % 2 == 0 else device + quarter

    def swapped(message, swap):
        return lax.ppermute(message, AXES, [(s, swap(s) % count) for s in range(count)])

    swaps = (next_chip, far_up, far_down, near)
    return [swapped(message, swap) for message, swap in zip(messages, swaps)]


def swapped_with(value, axis, partner):
    return lax.ppermute(value, axis, [(s, partner(s)) for s in range(lax.axis_size(axis))])


def summed_along_y(mine, theirs):
    half = mine + swapped_with(theirs, "c", lambda s: 1 - s)
    blocks = [half[k * QUARTER : (k + 1) * QUARTER] for k in range(4)]
    two = swapped_with(blocks[2], "y", lambda s: s ^ 2)
    three = swapped_with(blocks[3], "y", lambda s: s ^ 3)
    one = swapped_with(blocks[1], "y", lambda s: s ^ 1)
    return (blocks[0] + one) + (two + three)


def summed_along_z(total):
    three = swapped_with(total, "z", lambda s: s ^ 3)
    two = swapped_with(total, "z", lambda s: s ^ 2)
    one = swapped_with(total, "z", lambda s: s ^ 1)
    return (total + one) + (two + three)


def shared(total):
    two = swapped_with(total, "y", lambda s: s ^ 2)
    three = swapped_with(total, "y", lambda s: s ^ 3)
    one = swapped_with(total, "y", lambda s: s ^ 1)
    own = jnp.concatenate([total, one, two, three], axis=0)
    return own, swapped_with(own, "c", lambda s: 1 - s)


def body(
    node_features,
    edge_features,
    node_cotangent,
    edge_cotangent,
    edge_in_weight,
    edge_in_bias,
    edge_out_weight,
    edge_out_bias,
    node_in_weight,
    node_in_bias,
    node_out_weight,
    edge_ends,
    live_elements,
    shared_nodes,
    shared_counts,
    multiplicity,
):
    nodes, width = node_features.shape
    edges = edge_features.shape[0]
    devices = lax.axis_size(AXES)
    element_edges = edge_ends.shape[1]
    lists = shared_nodes.reshape(shared_nodes.shape[1:])
    copies = multiplicity.reshape(nodes // LANES, LANES)
    message = ((LANES, width), F32)
    node_f32 = ((nodes, width), F32)
    node_bf16 = ((nodes, width), BF16)
    both_f32 = ((element_edges, 2 * LANES), F32)
    both_bf16 = ((element_edges, 2 * LANES), BF16)
    edge_bf16 = ((edges, width), BF16)
    rows_height = padded(element_edges)
    ends_scratch = pltpu.VMEM((8, rows_height), jnp.int32)
    listed = 4 * LANES

    forward_args = in_hbm(
        shared_counts,
        edge_ends,
        lists,
        node_features,
        edge_features,
        edge_in_weight,
        edge_in_bias.reshape(1, -1),
        edge_out_weight,
        edge_out_bias.reshape(1, -1),
    )
    aggregate, *messages, edge_hidden, edge_slope, table, spread_target, pick = call(
        forward_kernel,
        [node_f32]
        + [message] * 4
        + [
            both_bf16,
            both_f32,
            ((element_edges, NPE), BF16),
            ((NPE, rows_height), BF16),
            ((listed, nodes), BF16),
        ],
        [HBM] * 9,
        [pltpu.SMEM(shared_counts.shape, jnp.int32)]
        + [pltpu.VMEM(arg.shape, arg.dtype) for arg in forward_args[1:]]
        + [
            pltpu.SemaphoreType.DMA((9,)),
            ends_scratch,
            pltpu.VMEM((rows_height, 2 * LANES), BF16),
            pltpu.VMEM((element_edges, NPE), BF16),
        ],
        forward_args,
        2_000_000_000,
        4_000_000,
    )
    arrived = exchanged(messages)
    spread_source, arrive, linear_part, hidden_back, node_cot, copies_wide = call(
        prepare_kernel,
        [
            ((NPE, rows_height), BF16),
            ((nodes, listed), BF16),
            node_f32,
            node_f32,
            node_bf16,
            node_f32,
        ],
        [SMEM, SMEM] + [VMEM] * 8,
        [ends_scratch],
        (
            shared_counts,
            live_elements,
            edge_ends,
            lists,
            copies,
            node_features,
            node_cotangent,
            node_in_weight,
            node_in_bias.reshape(1, -1),
            node_out_weight,
        ),
        1_000_000_000,
        4_000_000,
    )
    consistent_back, *messages, consistent, node_hidden, node_back = call(
        node_kernel,
        [node_f32] + [message] * 4 + [node_bf16] * 3,
        [VMEM] * 11,
        [],
        (
            aggregate,
            *arrived,
            arrive,
            pick,
            linear_part,
            hidden_back,
            copies_wide,
            node_in_weight,
        ),
        600_000_000,
        4_000_000,
    )
    arrived = exchanged(messages)
    node_part, node_terms, given, edges_across, nodes_across, sums_across, out_part, out_across = call(
        side_kernel,
        [
            node_f32,
            ((448, width), F32),
            both_bf16,
            ((2 * LANES, rows_height), BF16),
            ((width, nodes), BF16),
            ((2 * width, nodes), BF16),
            message,
            ((2 * LANES, 2 * LANES), BF16),
        ],
        [SMEM] + [VMEM] * 11,
        [],
        (
            live_elements,
            node_features,
            consistent,
            node_hidden,
            node_back,
            node_cot,
            node_in_weight,
            edge_features,
            edge_cotangent,
            edge_hidden,
            spread_target,
            edge_out_weight,
        ),
        1_000_000_000,
        4_000_000,
    )
    half_terms = ((4 * QUARTER, width), F32)
    edge_cot, edge_back, edge_sums, mine, theirs = call(
        backward_kernel,
        [
            both_f32,
            ((rows_height, 2 * LANES), BF16),
            ((nodes, 2 * LANES), F32),
            half_terms,
            half_terms,
        ],
        [VMEM] * 17,
        [pltpu.VMEM((8 * QUARTER, LANES), F32)],
        (
            consistent_back,
            *arrived,
            arrive,
            table,
            spread_source,
            spread_target,
            given,
            edge_slope,
            edges_across,
            nodes_across,
            sums_across,
            out_part,
            node_terms,
            out_across,
        ),
        2_000_000_000,
        6_000_000,
    )
    total = summed_along_y(mine, theirs)
    total = summed_along_z(total)
    total, edge_cot = lax.optimization_barrier((total, edge_cot))
    far = swapped_with(total, "z", lambda s: 7 - s)
    node_result, edge_result = call(
        results_kernel,
        [node_bf16, edge_bf16],
        [VMEM] * 5,
        [],
        (edge_cot, edge_back, edge_sums, node_part, edge_in_weight),
        2_000_000_000,
        6_000_000,
    )
    total, far, node_result = lax.optimization_barrier((total, far, node_result))
    own, other = shared(total + far)
    edge_scale = 1.0 / math.sqrt(edges * devices)
    node_scale = 1.0 / math.sqrt(nodes * devices)

    def finish(*refs):
        finish_kernel(edge_scale, node_scale, *refs)

    ei, eib, eo, eob, ni, nib, no, nob = call(
        finish,
        [
            ((384, width), F32),
            ((1, width), F32),
            ((128, width), F32),
            ((1, width), F32),
            ((256, width), F32),
            ((1, width), F32),
            ((128, width), F32),
            ((1, width), F32),
        ],
        [VMEM] * 2,
        [pltpu.VMEM((8 * QUARTER, LANES), F32)],
        (own, other),
        1_000_000,
        1_000_000,
    )
    return (
        node_result,
        edge_result,
        ei,
        eib.reshape(-1),
        eo,
        eob.reshape(-1),
        ni,
        nib.reshape(-1),
        no,
        nob.reshape(-1),
    )


def solution(mesh):
    grid = mesh.devices.reshape(8, 4, 2, 4)
    mesh = Mesh(grid, ("z", "y", "c", "rep"))
    rows = ("rep", "z", "y", "c")
    in_specs = (
        P(rows, None),
        P(rows, None),
        P(rows, None),
        P(rows, None),
        P(),
        P(),
        P(),
        P(),
        P(),
        P(),
        P(),
        P(),
        P(rows),
        P(rows, None, None),
        P(rows, None),
        P(rows),
    )
    out_specs = (
        P(rows, None),
        P(rows, None),
        P("rep", None),
        P("rep"),
        P("rep", None),
        P("rep"),
        P("rep", None),
        P("rep"),
        P("rep", None),
        P("rep"),
    )
    return jax.shard_map(body, mesh=mesh, in_specs=in_specs, out_specs=out_specs, check_vma=False)
```

```python
import math

import jax
import jax.numpy as jnp
from jax import lax
from jax.experimental import pallas as pl
from jax.experimental.pallas import tpu as pltpu
from jax.sharding import Mesh, PartitionSpec as P

NPE = 512
LANES = 128
BLOCK = 256
FORWARD_BLOCK = 1344
BACKWARD_BLOCK = 1344
QUARTER = 120
F32 = jnp.float32
BF16 = jnp.bfloat16
AXES = ("z", "y", "c")
VMEM = pl.BlockSpec(memory_space=pltpu.VMEM)
SMEM = pl.BlockSpec(memory_space=pltpu.SMEM)
HBM = pl.BlockSpec(memory_space=pltpu.HBM)


def padded(count):
    return -(-count // LANES) * LANES


def dot(left, right):
    return jnp.dot(left, right, preferred_element_type=F32)


def dot_t(left, right):
    return lax.dot_general(left, right, (((1,), (1,)), ((), ())), preferred_element_type=F32)


def dot_rows(left, right):
    return lax.dot_general(left, right, (((0,), (0,)), ((), ())), preferred_element_type=F32)


def split(value):
    high = value.astype(BF16)
    low = (value - high.astype(F32)).astype(BF16)
    return high, low


def as_column(row):
    return jnp.transpose(jnp.broadcast_to(row, (LANES, LANES)))


def hot(flags):
    return jnp.where(flags, jnp.ones(flags.shape, BF16), jnp.zeros(flags.shape, BF16))


def pick_table(row, width):
    column = as_column(row).astype(jnp.int16)
    lane = lax.broadcasted_iota(jnp.int32, (LANES, LANES), 1)
    tiles = [hot(column == (lane + start).astype(jnp.int16)) for start in range(0, width, LANES)]
    return jnp.concatenate(tiles, axis=1)


def spread_table(row, height):
    named = jnp.broadcast_to(row, (16, LANES)).astype(jnp.int16)
    named = jnp.concatenate([named] * (height // 16), axis=0)
    place = lax.broadcasted_iota(jnp.int32, (height, LANES), 0).astype(jnp.int16)
    return hot(place == named)


def list_rows(lists_ref, counts_ref):
    core = lax.axis_index("c")
    odd = lax.rem(lax.div(lax.axis_index("z"), 2), 2)
    lane = lax.broadcasted_iota(jnp.int32, (1, LANES), 1)
    rows = [jnp.where(lane < counts_ref[0, k], lists_ref[k : k + 1, :], -1) for k in range(4)]

    def ordered(flag, first, second):
        chosen = jnp.full((1, LANES), flag, jnp.int32) == 0
        return jnp.where(chosen, first, second), jnp.where(chosen, second, first)

    near, next_chip = ordered(core, rows[0], rows[1])
    up, down = ordered(odd, rows[2], rows[3])
    return (next_chip, up, down, near)


def outgoing(table_ref, values, refs):
    both = dot(table_ref[...], jnp.concatenate(split(values), axis=1))
    for k, ref in enumerate(refs):
        part = both[k * LANES : (k + 1) * LANES]
        ref[...] = part[:, :LANES] + part[:, LANES:]


def incoming(table_ref, refs):
    arrived = jnp.concatenate([ref[...] for ref in refs], axis=0)
    both = dot(table_ref[...], jnp.concatenate(split(arrived), axis=1))
    return both[:, :LANES] + both[:, LANES:]


def spans(count, block):
    return [(start, min(block, count - start)) for start in range(0, count, block)]


def blocks_of(count):
    return spans(count, BLOCK)


def twice(block):
    zero = jnp.zeros_like(block)
    return jnp.concatenate(
        [jnp.concatenate([block, zero], axis=1), jnp.concatenate([zero, block], axis=1)], axis=0
    )


def beside(ref, start, size, edges):
    return jnp.concatenate(
        [ref[start : start + size, :], ref[edges + start : edges + start + size, :]], axis=1
    )


def stage_ends(ends_ref, ends_sc):
    ends_sc[...] = jnp.full(ends_sc.shape, -1, jnp.int32)
    ends_sc[0:2, 0 : ends_ref.shape[1]] = ends_ref[...]


def edge_rows_table(ends_sc, side, start, size):
    parts = [
        pick_table(ends_sc[side : side + 1, first : first + LANES], NPE)
        for first in range(start, start + size, LANES)
    ]
    return jnp.concatenate(parts, axis=0)[:size]


def forward_kernel(
    counts_hbm, ends_hbm, lists_hbm, nf_hbm, ef_hbm, wi_hbm, bi_hbm, wo_hbm, bo_hbm,
    agg_ref, out0, out1, out2, out3, hid_ref, slope_ref, table_ref, spread_ref, pick_ref,
    counts_ref, ends_ref, lists_ref, nf_ref, ef_ref, wi_ref, bi_ref, wo_ref, bo_ref,
    sems, ends_sc, rows_sc, source_sc,
):
    pairs = (
        (ends_hbm, ends_ref),
        (nf_hbm, nf_ref),
        (wi_hbm, wi_ref),
        (ef_hbm, ef_ref),
        (bi_hbm, bi_ref),
        (wo_hbm, wo_ref),
        (bo_hbm, bo_ref),
        (lists_hbm, lists_ref),
        (counts_hbm, counts_ref),
    )
    loads = [
        pltpu.make_async_copy(source, target, sems.at[k])
        for k, (source, target) in enumerate(pairs)
    ]
    for load in loads:
        load.start()
    edges = ends_ref.shape[1]
    width = padded(edges)
    loads[0].wait()
    stage_ends(ends_ref, ends_sc)
    for first in range(0, width, LANES):
        spread_ref[:, first : first + LANES] = spread_table(
            ends_sc[1:2, first : first + LANES], NPE
        )
    for start, size in blocks_of(edges):
        source_sc[start : start + size, :] = edge_rows_table(ends_sc, 0, start, size)
        table_ref[start : start + size, :] = edge_rows_table(ends_sc, 1, start, size)
    rows_sc[edges:width, :] = jnp.zeros((width - edges, 2 * LANES), BF16)
    for load in loads[1:]:
        load.wait()
    values_rows = list_rows(lists_ref, counts_ref)
    for k, row in enumerate(values_rows):
        pick_ref[k * LANES : (k + 1) * LANES, :] = pick_table(row, nf_ref.shape[0])
    in_weights = jnp.concatenate([wi_ref[0:128, :], wi_ref[128:256, :]], axis=1)
    ends_rows = dot(nf_ref[...], in_weights).astype(BF16)
    source_rows = jnp.concatenate([ends_rows[:NPE, :LANES], ends_rows[NPE:, :LANES]], axis=1)
    target_rows = jnp.concatenate([ends_rows[:NPE, LANES:], ends_rows[NPE:, LANES:]], axis=1)
    own_weight = twice(wi_ref[256:384, :])
    out_weight = twice(wo_ref[...])
    in_bias = jnp.concatenate([bi_ref[...]] * 2, axis=1)
    out_bias = jnp.concatenate([bo_ref[...]] * 2, axis=1)
    for start, size in spans(edges, FORWARD_BLOCK):
        own = beside(ef_ref, start, size, edges)
        linear = (
            dot(source_sc[start : start + size, :], source_rows)
            + dot(table_ref[start : start + size, :], target_rows)
            + dot(own, own_weight)
            + in_bias
        )
        squashed = jax.nn.sigmoid(linear)
        hidden = (linear * squashed).astype(BF16)
        hid_ref[start : start + size, :] = hidden
        slope_ref[start : start + size, :] = squashed * (1.0 + linear * (1.0 - squashed))
        rows_sc[start : start + size, :] = (
            own.astype(F32) + dot(hidden, out_weight) + out_bias
        ).astype(BF16)
    sums = dot(spread_ref[...], rows_sc[...])
    agg_ref[0:NPE, :] = sums[:, :LANES]
    agg_ref[NPE:, :] = sums[:, LANES:]
    outgoing(pick_ref, agg_ref[...], (out0, out1, out2, out3))


def block_starts():
    core = lax.axis_index("c")
    place = lax.axis_index("y")
    starts = []
    for k in range(4):
        block = lax.bitwise_xor(place, k) * QUARTER
        kept = pl.multiple_of(core * (4 * QUARTER) + block, 8)
        sent = pl.multiple_of((1 - core) * (4 * QUARTER) + block, 8)
        starts.append((kept, sent))
    return starts


def prepare_kernel(
    counts_ref, live_ref, ends_ref, lists_ref, mult_ref, nf_ref, nc_ref, wn_ref, bn_ref, wo_ref,
    spread_ref, arrive_ref, linear_ref, hback_ref, cot_ref, shares_ref,
    ends_sc,
):
    nodes = nf_ref.shape[0]
    stage_ends(ends_ref, ends_sc)
    for first in range(0, ends_sc.shape[1], LANES):
        spread_ref[:, first : first + LANES] = spread_table(
            ends_sc[0:1, first : first + LANES], NPE
        )
    for k, row in enumerate(list_rows(lists_ref, counts_ref)):
        arrive_ref[:, k * LANES : (k + 1) * LANES] = spread_table(row, nodes)
    live = lax.broadcasted_iota(jnp.int32, (nodes, LANES), 0) < NPE * live_ref[0]
    cot = jnp.where(live, nc_ref[...].astype(F32), 0.0).astype(BF16)
    cot_ref[...] = cot
    linear_ref[...] = dot(nf_ref[...], wn_ref[0:128, :]) + bn_ref[...]
    hback_ref[...] = dot_t(cot, wo_ref[...])
    for b in range(nodes // LANES):
        shares_ref[b * LANES : (b + 1) * LANES, :] = 1.0 / as_column(mult_ref[b : b + 1, :].astype(F32))


def node_kernel(
    agg_ref, in0, in1, in2, in3, arrive_ref, pick_ref, linear_ref, hback_ref, shares_ref, wn_ref,
    cback_ref, out0, out1, out2, out3, cons_ref, hid_ref, back_ref,
):
    shares = shares_ref[...]
    total = agg_ref[...] + incoming(arrive_ref, (in0, in1, in2, in3))
    consistent = (total * shares).astype(BF16)
    linear = linear_ref[...] + dot(consistent, wn_ref[128:256, :])
    squashed = jax.nn.sigmoid(linear)
    slope = squashed * (1.0 + linear * (1.0 - squashed))
    back = (hback_ref[...] * slope).astype(BF16)
    consistent_back = dot_t(back, wn_ref[128:256, :]) * shares
    cback_ref[...] = consistent_back
    outgoing(pick_ref, consistent_back, (out0, out1, out2, out3))
    cons_ref[...] = consistent
    hid_ref[...] = (linear * squashed).astype(BF16)
    back_ref[...] = back


def side_kernel(
    live_ref, nf_ref, cons_ref, hid_ref, back_ref, cot_ref, wn_ref, ef_ref, ec_ref, ehid_ref,
    spread_ref, wo_ref, part_ref, terms_ref, given_ref, eft_ref, nft_ref, hsumt_ref, outw_ref, wot_ref,
):
    back = back_ref[...]
    cot_half = cot_ref[...]
    cot = cot_half.astype(F32)
    part_ref[...] = cot + dot_t(back, wn_ref[0:128, :])
    terms_ref[0:128, :] = dot_rows(nf_ref[...], back)
    terms_ref[128:256, :] = dot_rows(cons_ref[...], back)
    terms_ref[256:384, :] = dot_rows(hid_ref[...], cot_half)
    terms_ref[384:448, :] = jnp.zeros((64, LANES), F32)
    terms_ref[386:387, :] = jnp.sum(back.astype(F32), axis=0, keepdims=True)
    terms_ref[387:388, :] = jnp.sum(cot, axis=0, keepdims=True)
    edges = ef_ref.shape[0] // 2
    live = jnp.full((edges, LANES), live_ref[0], jnp.int32)
    width = eft_ref.shape[1]
    for slot in range(2):
        rows = slice(slot * edges, (slot + 1) * edges)
        lanes = slice(slot * LANES, (slot + 1) * LANES)
        given_ref[:, lanes] = jnp.where(live > slot, ec_ref[rows, :].astype(F32), 0.0).astype(BF16)
        eft_ref[lanes, 0:edges] = jnp.transpose(ef_ref[rows, :].astype(F32)).astype(BF16)
    eft_ref[:, edges:] = jnp.zeros((2 * LANES, width - edges), BF16)
    nft_ref[...] = jnp.transpose(nf_ref[...].astype(F32)).astype(BF16)
    hidden = ehid_ref[...]
    filler = jnp.zeros((width - edges, 2 * LANES), BF16)
    sums = dot(spread_ref[...], jnp.concatenate([hidden, filler], axis=0))
    for slot in range(2):
        lanes = slice(slot * LANES, (slot + 1) * LANES)
        high, low = split(jnp.transpose(sums[:, lanes]))
        hsumt_ref[0:LANES, slot * NPE : (slot + 1) * NPE] = high
        hsumt_ref[LANES:, slot * NPE : (slot + 1) * NPE] = low
    both = dot_rows(hidden, given_ref[...])
    outw_ref[...] = both[:LANES, :LANES] + both[LANES:, LANES:]
    wot_ref[...] = twice(jnp.transpose(wo_ref[...].astype(F32)).astype(BF16))


def backward_kernel(
    cback_ref, in0, in1, in2, in3, arrive_ref, table_ref, spread_s_ref, spread_t_ref,
    given_ref, slope_ref, eft_ref, nft_ref, hsumt_ref, outw_ref, terms_ref, wot_ref,
    cot_ref, eback_ref, sums_ref, mine_ref, theirs_ref,
    terms_sc,
):
    edges = table_ref.shape[0]
    width = padded(edges)
    agg_back = (cback_ref[...] + incoming(arrive_ref, (in0, in1, in2, in3))).astype(BF16)
    table_rows = jnp.concatenate([agg_back[:NPE], agg_back[NPE:]], axis=1)
    in_bias = jnp.zeros((1, 2 * LANES), F32)
    out_bias = jnp.zeros((1, 2 * LANES), F32)
    for start, size in spans(edges, BACKWARD_BLOCK):
        rows = slice(start, start + size)
        cot = given_ref[rows, :].astype(F32) + dot(table_ref[rows, :], table_rows)
        half = cot.astype(BF16)
        back = (dot(half, wot_ref[...]) * slope_ref[rows, :]).astype(BF16)
        cot_ref[rows, :] = cot
        eback_ref[rows, :] = back
        in_bias = in_bias + jnp.sum(back.astype(F32), axis=0, keepdims=True)
        out_bias = out_bias + jnp.sum(half.astype(F32), axis=0, keepdims=True)
    eback_ref[edges:width, :] = jnp.zeros((width - edges, 2 * LANES), BF16)
    by_source = dot(spread_s_ref[...], eback_ref[...])
    by_target = dot(spread_t_ref[...], eback_ref[...])
    by_edge = dot(eft_ref[...], eback_ref[...])
    sums_ref[0:NPE, 0:LANES] = by_source[:, :LANES]
    sums_ref[NPE : 2 * NPE, 0:LANES] = by_source[:, LANES:]
    sums_ref[0:NPE, LANES:] = by_target[:, :LANES]
    sums_ref[NPE : 2 * NPE, LANES:] = by_target[:, LANES:]
    both = dot(nft_ref[...], jnp.concatenate(split(sums_ref[...]), axis=1))
    terms_sc[0:128, :] = both[:, 0:128] + both[:, 256:384]
    terms_sc[128:256, :] = both[:, 128:256] + both[:, 384:512]
    terms_sc[256:384, :] = by_edge[:LANES, :LANES] + by_edge[LANES:, LANES:]
    shared_part = dot(hsumt_ref[...], agg_back)
    terms_sc[384:512, :] = outw_ref[...] + (shared_part[:LANES] + shared_part[LANES:])
    terms_sc[512:960, :] = terms_ref[...]
    terms_sc[896:897, :] = in_bias[:, :LANES] + in_bias[:, LANES:]
    terms_sc[897:898, :] = out_bias[:, :LANES] + out_bias[:, LANES:]
    for k, (kept, sent) in enumerate(block_starts()):
        mine_ref[k * QUARTER : (k + 1) * QUARTER, :] = terms_sc[pl.ds(kept, QUARTER), :]
        theirs_ref[k * QUARTER : (k + 1) * QUARTER, :] = terms_sc[pl.ds(sent, QUARTER), :]


def results_kernel(cot_ref, eback_ref, sums_ref, part_ref, wi_ref, node_ref, edge_ref):
    high, low = split(sums_ref[...])
    node_ref[...] = (
        part_ref[...]
        + (dot_t(high[:, :LANES], wi_ref[0:128, :]) + dot_t(low[:, :LANES], wi_ref[0:128, :]))
        + (dot_t(high[:, LANES:], wi_ref[128:256, :]) + dot_t(low[:, LANES:], wi_ref[128:256, :]))
    ).astype(BF16)
    edges = cot_ref.shape[0]
    own_weight = twice(jnp.transpose(wi_ref[256:384, :].astype(F32)).astype(BF16))
    result = (cot_ref[...] + dot(eback_ref[0:edges, :], own_weight)).astype(BF16)
    edge_ref[0:edges, :] = result[:, :LANES]
    edge_ref[edges:, :] = result[:, LANES:]


def finish_kernel(
    edge_scale, node_scale, own_ref, other_ref, ei, eib, eo, eob, ni, nib, no, nob, sums_sc
):
    for k, (kept, sent) in enumerate(block_starts()):
        sums_sc[pl.ds(kept, QUARTER), :] = own_ref[k * QUARTER : (k + 1) * QUARTER, :]
        sums_sc[pl.ds(sent, QUARTER), :] = other_ref[k * QUARTER : (k + 1) * QUARTER, :]
    ei[...] = sums_sc[0:384, :] * edge_scale
    eo[...] = sums_sc[384:512, :] * edge_scale
    ni[...] = sums_sc[512:768, :] * node_scale
    no[...] = sums_sc[768:896, :] * node_scale
    eib[...] = sums_sc[896:897, :] * edge_scale
    eob[...] = sums_sc[897:898, :] * edge_scale
    nib[...] = sums_sc[898:899, :] * node_scale
    nob[...] = sums_sc[899:900, :] * node_scale


def call(kernel, out_shapes, specs, scratch, args, flops, moved):
    return pl.pallas_call(
        kernel,
        out_shape=[jax.ShapeDtypeStruct(shape, dtype) for shape, dtype in out_shapes],
        in_specs=specs,
        out_specs=[VMEM] * len(out_shapes),
        scratch_shapes=scratch,
        compiler_params=pltpu.CompilerParams(vmem_limit_bytes=40 * 1024 * 1024),
        cost_estimate=pl.CostEstimate(flops=flops, bytes_accessed=moved, transcendentals=0),
    )(*args)


def in_hbm(*values):
    return tuple(pltpu.with_memory_space_constraint(value, pltpu.HBM) for value in values)


def exchanged(messages):
    def near(device):
        return device ^ 1

    def next_chip(device):
        return device + 1 if device % 2 else device - 1

    count = lax.axis_size(AXES)
    quarter = count // 4

    def far_up(device):
        return device + quarter if (device // quarter) % 2 == 0 else device - quarter

    def far_down(device):
        return device - quarter if (device // quarter) % 2 == 0 else device + quarter

    def swapped(message, swap):
        return lax.ppermute(message, AXES, [(s, swap(s) % count) for s in range(count)])

    swaps = (next_chip, far_up, far_down, near)
    return [swapped(message, swap) for message, swap in zip(messages, swaps)]


def swapped_with(value, axis, partner):
    return lax.ppermute(value, axis, [(s, partner(s)) for s in range(lax.axis_size(axis))])


def summed_along_y(mine, theirs):
    half = mine + swapped_with(theirs, "c", lambda s: 1 - s)
    blocks = [half[k * QUARTER : (k + 1) * QUARTER] for k in range(4)]
    one = swapped_with(blocks[1], "y", lambda s: s ^ 1)
    three = swapped_with(blocks[3], "y", lambda s: s ^ 3)
    two = swapped_with(blocks[2], "y", lambda s: s ^ 2)
    one, three, two = lax.optimization_barrier((one, three, two))
    return (blocks[0] + one) + (two + three)


def summed_along_z(total):
    one = swapped_with(total, "z", lambda s: s ^ 1)
    three = swapped_with(total, "z", lambda s: s ^ 3)
    two = swapped_with(total, "z", lambda s: s ^ 2)
    one, three, two = lax.optimization_barrier((one, three, two))
    return (total + one) + (two + three)


def shared(total):
    one = swapped_with(total, "y", lambda s: s ^ 1)
    three = swapped_with(total, "y", lambda s: s ^ 3)
    two = swapped_with(total, "y", lambda s: s ^ 2)
    one, three, two = lax.optimization_barrier((one, three, two))
    own = jnp.concatenate([total, one, two, three], axis=0)
    return own, swapped_with(own, "c", lambda s: 1 - s)


def body(
    node_features,
    edge_features,
    node_cotangent,
    edge_cotangent,
    edge_in_weight,
    edge_in_bias,
    edge_out_weight,
    edge_out_bias,
    node_in_weight,
    node_in_bias,
    node_out_weight,
    edge_ends,
    live_elements,
    shared_nodes,
    shared_counts,
    multiplicity,
):
    nodes, width = node_features.shape
    edges = edge_features.shape[0]
    devices = lax.axis_size(AXES)
    element_edges = edge_ends.shape[1]
    lists = shared_nodes.reshape(shared_nodes.shape[1:])
    copies = multiplicity.reshape(nodes // LANES, LANES)
    message = ((LANES, width), F32)
    node_f32 = ((nodes, width), F32)
    node_bf16 = ((nodes, width), BF16)
    both_f32 = ((element_edges, 2 * LANES), F32)
    both_bf16 = ((element_edges, 2 * LANES), BF16)
    edge_bf16 = ((edges, width), BF16)
    rows_height = padded(element_edges)
    ends_scratch = pltpu.VMEM((8, rows_height), jnp.int32)
    listed = 4 * LANES

    forward_args = in_hbm(
        shared_counts,
        edge_ends,
        lists,
        node_features,
        edge_features,
        edge_in_weight,
        edge_in_bias.reshape(1, -1),
        edge_out_weight,
        edge_out_bias.reshape(1, -1),
    )
    aggregate, *messages, edge_hidden, edge_slope, table, spread_target, pick = call(
        forward_kernel,
        [node_f32]
        + [message] * 4
        + [
            both_bf16,
            both_f32,
            ((element_edges, NPE), BF16),
            ((NPE, rows_height), BF16),
            ((listed, nodes), BF16),
        ],
        [HBM] * 9,
        [pltpu.SMEM(shared_counts.shape, jnp.int32)]
        + [pltpu.VMEM(arg.shape, arg.dtype) for arg in forward_args[1:]]
        + [
            pltpu.SemaphoreType.DMA((9,)),
            ends_scratch,
            pltpu.VMEM((rows_height, 2 * LANES), BF16),
            pltpu.VMEM((element_edges, NPE), BF16),
        ],
        forward_args,
        2_000_000_000,
        4_000_000,
    )
    arrived = exchanged(messages)
    spread_source, arrive, linear_part, hidden_back, node_cot, node_shares = call(
        prepare_kernel,
        [
            ((NPE, rows_height), BF16),
            ((nodes, listed), BF16),
            node_f32,
            node_f32,
            node_bf16,
            node_f32,
        ],
        [SMEM, SMEM] + [VMEM] * 8,
        [ends_scratch],
        (
            shared_counts,
            live_elements,
            edge_ends,
            lists,
            copies,
            node_features,
            node_cotangent,
            node_in_weight,
            node_in_bias.reshape(1, -1),
            node_out_weight,
        ),
        1_000_000_000,
        4_000_000,
    )
    consistent_back, *messages, consistent, node_hidden, node_back = call(
        node_kernel,
        [node_f32] + [message] * 4 + [node_bf16] * 3,
        [VMEM] * 11,
        [],
        (
            aggregate,
            *arrived,
            arrive,
            pick,
            linear_part,
            hidden_back,
            node_shares,
            node_in_weight,
        ),
        600_000_000,
        4_000_000,
    )
    arrived = exchanged(messages)
    node_part, node_terms, given, edges_across, nodes_across, sums_across, out_part, out_across = call(
        side_kernel,
        [
            node_f32,
            ((448, width), F32),
            both_bf16,
            ((2 * LANES, rows_height), BF16),
            ((width, nodes), BF16),
            ((2 * width, nodes), BF16),
            message,
            ((2 * LANES, 2 * LANES), BF16),
        ],
        [SMEM] + [VMEM] * 11,
        [],
        (
            live_elements,
            node_features,
            consistent,
            node_hidden,
            node_back,
            node_cot,
            node_in_weight,
            edge_features,
            edge_cotangent,
            edge_hidden,
            spread_target,
            edge_out_weight,
        ),
        1_000_000_000,
        4_000_000,
    )
    half_terms = ((4 * QUARTER, width), F32)
    edge_cot, edge_back, edge_sums, mine, theirs = call(
        backward_kernel,
        [
            both_f32,
            ((rows_height, 2 * LANES), BF16),
            ((nodes, 2 * LANES), F32),
            half_terms,
            half_terms,
        ],
        [VMEM] * 17,
        [pltpu.VMEM((8 * QUARTER, LANES), F32)],
        (
            consistent_back,
            *arrived,
            arrive,
            table,
            spread_source,
            spread_target,
            given,
            edge_slope,
            edges_across,
            nodes_across,
            sums_across,
            out_part,
            node_terms,
            out_across,
        ),
        2_000_000_000,
        6_000_000,
    )
    total = summed_along_y(mine, theirs)
    total = summed_along_z(total)
    total, edge_cot = lax.optimization_barrier((total, edge_cot))
    far = swapped_with(total, "z", lambda s: 7 - s)
    node_result, edge_result = call(
        results_kernel,
        [node_bf16, edge_bf16],
        [VMEM] * 5,
        [],
        (edge_cot, edge_back, edge_sums, node_part, edge_in_weight),
        2_000_000_000,
        6_000_000,
    )
    total, far, node_result = lax.optimization_barrier((total, far, node_result))
    own, other = shared(total + far)
    edge_scale = 1.0 / math.sqrt(edges * devices)
    node_scale = 1.0 / math.sqrt(nodes * devices)

    def finish(*refs):
        finish_kernel(edge_scale, node_scale, *refs)

    ei, eib, eo, eob, ni, nib, no, nob = call(
        finish,
        [
            ((384, width), F32),
            ((1, width), F32),
            ((128, width), F32),
            ((1, width), F32),
            ((256, width), F32),
            ((1, width), F32),
            ((128, width), F32),
            ((1, width), F32),
        ],
        [VMEM] * 2,
        [pltpu.VMEM((8 * QUARTER, LANES), F32)],
        (own, other),
        1_000_000,
        1_000_000,
    )
    return (
        node_result,
        edge_result,
        ei,
        eib.reshape(-1),
        eo,
        eob.reshape(-1),
        ni,
        nib.reshape(-1),
        no,
        nob.reshape(-1),
    )


def solution(mesh):
    grid = mesh.devices.reshape(8, 4, 2, 4)
    mesh = Mesh(grid, ("z", "y", "c", "rep"))
    rows = ("rep", "z", "y", "c")
    in_specs = (
        P(rows, None),
        P(rows, None),
        P(rows, None),
        P(rows, None),
        P(),
        P(),
        P(),
        P(),
        P(),
        P(),
        P(),
        P(),
        P(rows),
        P(rows, None, None),
        P(rows, None),
        P(rows),
    )
    out_specs = (
        P(rows, None),
        P(rows, None),
        P("rep", None),
        P("rep"),
        P("rep", None),
        P("rep"),
        P("rep", None),
        P("rep"),
        P("rep", None),
        P("rep"),
    )
    return jax.shard_map(body, mesh=mesh, in_specs=in_specs, out_specs=out_specs, check_vma=False)
```

```python
import math

import jax
import jax.numpy as jnp
from jax import lax
from jax.experimental import pallas as pl
from jax.experimental.pallas import tpu as pltpu
from jax.sharding import Mesh, PartitionSpec as P

NPE = 512
LANES = 128
BLOCK = 256
FORWARD_BLOCK = 1344
BACKWARD_BLOCK = 1344
QUARTER = 120
F32 = jnp.float32
BF16 = jnp.bfloat16
AXES = ("z", "y", "c")
VMEM = pl.BlockSpec(memory_space=pltpu.VMEM)
SMEM = pl.BlockSpec(memory_space=pltpu.SMEM)
HBM = pl.BlockSpec(memory_space=pltpu.HBM)


def padded(count):
    return -(-count // LANES) * LANES


def dot(left, right):
    return jnp.dot(left, right, preferred_element_type=F32)


def dot_t(left, right):
    return lax.dot_general(left, right, (((1,), (1,)), ((), ())), preferred_element_type=F32)


def dot_rows(left, right):
    return lax.dot_general(left, right, (((0,), (0,)), ((), ())), preferred_element_type=F32)


def split(value):
    high = value.astype(BF16)
    low = (value - high.astype(F32)).astype(BF16)
    return high, low


def as_column(row):
    return jnp.transpose(jnp.broadcast_to(row, (LANES, LANES)))


def hot(flags):
    return jnp.where(flags, jnp.ones(flags.shape, BF16), jnp.zeros(flags.shape, BF16))


def pick_table(row, width):
    column = as_column(row).astype(jnp.int16)
    lane = lax.broadcasted_iota(jnp.int32, (LANES, LANES), 1)
    tiles = [hot(column == (lane + start).astype(jnp.int16)) for start in range(0, width, LANES)]
    return jnp.concatenate(tiles, axis=1)


def spread_table(row, height):
    named = jnp.broadcast_to(row, (16, LANES)).astype(jnp.int16)
    named = jnp.concatenate([named] * (height // 16), axis=0)
    place = lax.broadcasted_iota(jnp.int32, (height, LANES), 0).astype(jnp.int16)
    return hot(place == named)


def list_rows(lists_ref, counts_ref):
    core = lax.axis_index("c")
    odd = lax.rem(lax.div(lax.axis_index("z"), 2), 2)
    lane = lax.broadcasted_iota(jnp.int32, (1, LANES), 1)
    rows = [jnp.where(lane < counts_ref[0, k], lists_ref[k : k + 1, :], -1) for k in range(4)]

    def ordered(flag, first, second):
        chosen = jnp.full((1, LANES), flag, jnp.int32) == 0
        return jnp.where(chosen, first, second), jnp.where(chosen, second, first)

    near, next_chip = ordered(core, rows[0], rows[1])
    up, down = ordered(odd, rows[2], rows[3])
    return (next_chip, up, down, near)


def outgoing(table_ref, values, refs):
    picked = dot(table_ref[...], values.astype(BF16))
    for k, ref in enumerate(refs):
        ref[...] = picked[k * LANES : (k + 1) * LANES]


def incoming(table_ref, refs):
    arrived = jnp.concatenate([ref[...] for ref in refs], axis=0)
    return dot(table_ref[...], arrived.astype(BF16))


def spans(count, block):
    return [(start, min(block, count - start)) for start in range(0, count, block)]


def blocks_of(count):
    return spans(count, BLOCK)


def twice(block):
    zero = jnp.zeros_like(block)
    return jnp.concatenate(
        [jnp.concatenate([block, zero], axis=1), jnp.concatenate([zero, block], axis=1)], axis=0
    )


def beside(ref, start, size, edges):
    return jnp.concatenate(
        [ref[start : start + size, :], ref[edges + start : edges + start + size, :]], axis=1
    )


def stage_ends(ends_ref, ends_sc):
    ends_sc[...] = jnp.full(ends_sc.shape, -1, jnp.int32)
    ends_sc[0:2, 0 : ends_ref.shape[1]] = ends_ref[...]


def edge_rows_table(ends_sc, side, start, size):
    parts = [
        pick_table(ends_sc[side : side + 1, first : first + LANES], NPE)
        for first in range(start, start + size, LANES)
    ]
    return jnp.concatenate(parts, axis=0)[:size]


def forward_kernel(
    counts_hbm, ends_hbm, lists_hbm, nf_hbm, ef_hbm, wi_hbm, bi_hbm, wo_hbm, bo_hbm,
    agg_ref, out0, out1, out2, out3, hid_ref, slope_ref, table_ref, spread_ref, pick_ref,
    counts_ref, ends_ref, lists_ref, nf_ref, ef_ref, wi_ref, bi_ref, wo_ref, bo_ref,
    sems, ends_sc, rows_sc, source_sc,
):
    pairs = (
        (ends_hbm, ends_ref),
        (nf_hbm, nf_ref),
        (wi_hbm, wi_ref),
        (ef_hbm, ef_ref),
        (bi_hbm, bi_ref),
        (wo_hbm, wo_ref),
        (bo_hbm, bo_ref),
        (lists_hbm, lists_ref),
        (counts_hbm, counts_ref),
    )
    loads = [
        pltpu.make_async_copy(source, target, sems.at[k])
        for k, (source, target) in enumerate(pairs)
    ]
    for load in loads:
        load.start()
    edges = ends_ref.shape[1]
    width = padded(edges)
    loads[0].wait()
    stage_ends(ends_ref, ends_sc)
    for first in range(0, width, LANES):
        spread_ref[:, first : first + LANES] = spread_table(
            ends_sc[1:2, first : first + LANES], NPE
        )
    for start, size in blocks_of(edges):
        source_sc[start : start + size, :] = edge_rows_table(ends_sc, 0, start, size)
        table_ref[start : start + size, :] = edge_rows_table(ends_sc, 1, start, size)
    rows_sc[edges:width, :] = jnp.zeros((width - edges, 2 * LANES), BF16)
    for load in loads[1:]:
        load.wait()
    values_rows = list_rows(lists_ref, counts_ref)
    for k, row in enumerate(values_rows):
        pick_ref[k * LANES : (k + 1) * LANES, :] = pick_table(row, nf_ref.shape[0])
    in_weights = jnp.concatenate([wi_ref[0:128, :], wi_ref[128:256, :]], axis=1)
    ends_rows = dot(nf_ref[...], in_weights).astype(BF16)
    source_rows = jnp.concatenate([ends_rows[:NPE, :LANES], ends_rows[NPE:, :LANES]], axis=1)
    target_rows = jnp.concatenate([ends_rows[:NPE, LANES:], ends_rows[NPE:, LANES:]], axis=1)
    own_weight = twice(wi_ref[256:384, :])
    out_weight = twice(wo_ref[...])
    in_bias = jnp.concatenate([bi_ref[...]] * 2, axis=1)
    out_bias = jnp.concatenate([bo_ref[...]] * 2, axis=1)
    for start, size in spans(edges, FORWARD_BLOCK):
        own = beside(ef_ref, start, size, edges)
        linear = (
            dot(source_sc[start : start + size, :], source_rows)
            + dot(table_ref[start : start + size, :], target_rows)
            + dot(own, own_weight)
            + in_bias
        )
        squashed = jax.nn.sigmoid(linear)
        hidden = (linear * squashed).astype(BF16)
        hid_ref[start : start + size, :] = hidden
        slope_ref[start : start + size, :] = squashed * (1.0 + linear * (1.0 - squashed))
        rows_sc[start : start + size, :] = (
            own.astype(F32) + dot(hidden, out_weight) + out_bias
        ).astype(BF16)
    sums = dot(spread_ref[...], rows_sc[...])
    agg_ref[0:NPE, :] = sums[:, :LANES]
    agg_ref[NPE:, :] = sums[:, LANES:]
    outgoing(pick_ref, agg_ref[...], (out0, out1, out2, out3))


def block_starts():
    core = lax.axis_index("c")
    place = lax.axis_index("y")
    starts = []
    for k in range(4):
        block = lax.bitwise_xor(place, k) * QUARTER
        kept = pl.multiple_of(core * (4 * QUARTER) + block, 8)
        sent = pl.multiple_of((1 - core) * (4 * QUARTER) + block, 8)
        starts.append((kept, sent))
    return starts


def prepare_kernel(
    counts_ref, live_ref, ends_ref, lists_ref, mult_ref, nf_ref, nc_ref, wn_ref, bn_ref, wo_ref,
    spread_ref, arrive_ref, linear_ref, hback_ref, cot_ref, shares_ref,
    ends_sc,
):
    nodes = nf_ref.shape[0]
    stage_ends(ends_ref, ends_sc)
    for first in range(0, ends_sc.shape[1], LANES):
        spread_ref[:, first : first + LANES] = spread_table(
            ends_sc[0:1, first : first + LANES], NPE
        )
    for k, row in enumerate(list_rows(lists_ref, counts_ref)):
        arrive_ref[:, k * LANES : (k + 1) * LANES] = spread_table(row, nodes)
    live = lax.broadcasted_iota(jnp.int32, (nodes, LANES), 0) < NPE * live_ref[0]
    cot = jnp.where(live, nc_ref[...].astype(F32), 0.0).astype(BF16)
    cot_ref[...] = cot
    linear_ref[...] = dot(nf_ref[...], wn_ref[0:128, :]) + bn_ref[...]
    hback_ref[...] = dot_t(cot, wo_ref[...])
    for b in range(nodes // LANES):
        shares_ref[b * LANES : (b + 1) * LANES, :] = 1.0 / as_column(mult_ref[b : b + 1, :].astype(F32))


def node_kernel(
    agg_ref, in0, in1, in2, in3, arrive_ref, pick_ref, linear_ref, hback_ref, shares_ref, wn_ref,
    cback_ref, out0, out1, out2, out3, cons_ref, hid_ref, back_ref,
):
    shares = shares_ref[...]
    total = agg_ref[...] + incoming(arrive_ref, (in0, in1, in2, in3))
    consistent = (total * shares).astype(BF16)
    linear = linear_ref[...] + dot(consistent, wn_ref[128:256, :])
    squashed = jax.nn.sigmoid(linear)
    slope = squashed * (1.0 + linear * (1.0 - squashed))
    back = (hback_ref[...] * slope).astype(BF16)
    consistent_back = dot_t(back, wn_ref[128:256, :]) * shares
    cback_ref[...] = consistent_back
    outgoing(pick_ref, consistent_back, (out0, out1, out2, out3))
    cons_ref[...] = consistent
    hid_ref[...] = (linear * squashed).astype(BF16)
    back_ref[...] = back


def side_kernel(
    live_ref, nf_ref, cons_ref, hid_ref, back_ref, cot_ref, wn_ref, ef_ref, ec_ref, ehid_ref,
    spread_ref, wo_ref, part_ref, terms_ref, given_ref, eft_ref, nft_ref, hsumt_ref, outw_ref, wot_ref,
):
    back = back_ref[...]
    cot_half = cot_ref[...]
    cot = cot_half.astype(F32)
    part_ref[...] = cot + dot_t(back, wn_ref[0:128, :])
    terms_ref[0:128, :] = dot_rows(nf_ref[...], back)
    terms_ref[128:256, :] = dot_rows(cons_ref[...], back)
    terms_ref[256:384, :] = dot_rows(hid_ref[...], cot_half)
    terms_ref[384:448, :] = jnp.zeros((64, LANES), F32)
    terms_ref[386:387, :] = jnp.sum(back.astype(F32), axis=0, keepdims=True)
    terms_ref[387:388, :] = jnp.sum(cot, axis=0, keepdims=True)
    edges = ef_ref.shape[0] // 2
    live = jnp.full((edges, LANES), live_ref[0], jnp.int32)
    width = eft_ref.shape[1]
    for slot in range(2):
        rows = slice(slot * edges, (slot + 1) * edges)
        lanes = slice(slot * LANES, (slot + 1) * LANES)
        given_ref[:, lanes] = jnp.where(live > slot, ec_ref[rows, :].astype(F32), 0.0).astype(BF16)
        eft_ref[lanes, 0:edges] = jnp.transpose(ef_ref[rows, :].astype(F32)).astype(BF16)
    eft_ref[:, edges:] = jnp.zeros((2 * LANES, width - edges), BF16)
    nft_ref[...] = jnp.transpose(nf_ref[...].astype(F32)).astype(BF16)
    hidden = ehid_ref[...]
    filler = jnp.zeros((width - edges, 2 * LANES), BF16)
    sums = dot(spread_ref[...], jnp.concatenate([hidden, filler], axis=0))
    for slot in range(2):
        lanes = slice(slot * LANES, (slot + 1) * LANES)
        high, low = split(jnp.transpose(sums[:, lanes]))
        hsumt_ref[0:LANES, slot * NPE : (slot + 1) * NPE] = high
        hsumt_ref[LANES:, slot * NPE : (slot + 1) * NPE] = low
    both = dot_rows(hidden, given_ref[...])
    outw_ref[...] = both[:LANES, :LANES] + both[LANES:, LANES:]
    wot_ref[...] = twice(jnp.transpose(wo_ref[...].astype(F32)).astype(BF16))


def backward_kernel(
    cback_ref, in0, in1, in2, in3, arrive_ref, table_ref, spread_s_ref, spread_t_ref,
    given_ref, slope_ref, eft_ref, nft_ref, hsumt_ref, outw_ref, terms_ref, wot_ref,
    cot_ref, eback_ref, sums_ref, mine_ref, theirs_ref,
    terms_sc,
):
    edges = table_ref.shape[0]
    width = padded(edges)
    agg_back = (cback_ref[...] + incoming(arrive_ref, (in0, in1, in2, in3))).astype(BF16)
    table_rows = jnp.concatenate([agg_back[:NPE], agg_back[NPE:]], axis=1)
    in_bias = jnp.zeros((1, 2 * LANES), F32)
    out_bias = jnp.zeros((1, 2 * LANES), F32)
    for start, size in spans(edges, BACKWARD_BLOCK):
        rows = slice(start, start + size)
        cot = given_ref[rows, :].astype(F32) + dot(table_ref[rows, :], table_rows)
        half = cot.astype(BF16)
        back = (dot(half, wot_ref[...]) * slope_ref[rows, :]).astype(BF16)
        cot_ref[rows, :] = cot
        eback_ref[rows, :] = back
        in_bias = in_bias + jnp.sum(back.astype(F32), axis=0, keepdims=True)
        out_bias = out_bias + jnp.sum(half.astype(F32), axis=0, keepdims=True)
    eback_ref[edges:width, :] = jnp.zeros((width - edges, 2 * LANES), BF16)
    by_source = dot(spread_s_ref[...], eback_ref[...])
    by_target = dot(spread_t_ref[...], eback_ref[...])
    by_edge = dot(eft_ref[...], eback_ref[...])
    sums_ref[0:NPE, 0:LANES] = by_source[:, :LANES]
    sums_ref[NPE : 2 * NPE, 0:LANES] = by_source[:, LANES:]
    sums_ref[0:NPE, LANES:] = by_target[:, :LANES]
    sums_ref[NPE : 2 * NPE, LANES:] = by_target[:, LANES:]
    both = dot(nft_ref[...], jnp.concatenate(split(sums_ref[...]), axis=1))
    terms_sc[0:128, :] = both[:, 0:128] + both[:, 256:384]
    terms_sc[128:256, :] = both[:, 128:256] + both[:, 384:512]
    terms_sc[256:384, :] = by_edge[:LANES, :LANES] + by_edge[LANES:, LANES:]
    shared_part = dot(hsumt_ref[...], agg_back)
    terms_sc[384:512, :] = outw_ref[...] + (shared_part[:LANES] + shared_part[LANES:])
    terms_sc[512:960, :] = terms_ref[...]
    terms_sc[896:897, :] = in_bias[:, :LANES] + in_bias[:, LANES:]
    terms_sc[897:898, :] = out_bias[:, :LANES] + out_bias[:, LANES:]
    for k, (kept, sent) in enumerate(block_starts()):
        mine_ref[k * QUARTER : (k + 1) * QUARTER, :] = terms_sc[pl.ds(kept, QUARTER), :]
        theirs_ref[k * QUARTER : (k + 1) * QUARTER, :] = terms_sc[pl.ds(sent, QUARTER), :]


def results_kernel(cot_ref, eback_ref, sums_ref, part_ref, wi_ref, node_ref, edge_ref):
    high, low = split(sums_ref[...])
    node_ref[...] = (
        part_ref[...]
        + (dot_t(high[:, :LANES], wi_ref[0:128, :]) + dot_t(low[:, :LANES], wi_ref[0:128, :]))
        + (dot_t(high[:, LANES:], wi_ref[128:256, :]) + dot_t(low[:, LANES:], wi_ref[128:256, :]))
    ).astype(BF16)
    edges = cot_ref.shape[0]
    own_weight = twice(jnp.transpose(wi_ref[256:384, :].astype(F32)).astype(BF16))
    result = (cot_ref[...] + dot(eback_ref[0:edges, :], own_weight)).astype(BF16)
    edge_ref[0:edges, :] = result[:, :LANES]
    edge_ref[edges:, :] = result[:, LANES:]


def finish_kernel(
    edge_scale, node_scale, own_ref, other_ref, ei, eib, eo, eob, ni, nib, no, nob, sums_sc
):
    for k, (kept, sent) in enumerate(block_starts()):
        sums_sc[pl.ds(kept, QUARTER), :] = own_ref[k * QUARTER : (k + 1) * QUARTER, :]
        sums_sc[pl.ds(sent, QUARTER), :] = other_ref[k * QUARTER : (k + 1) * QUARTER, :]
    ei[...] = sums_sc[0:384, :] * edge_scale
    eo[...] = sums_sc[384:512, :] * edge_scale
    ni[...] = sums_sc[512:768, :] * node_scale
    no[...] = sums_sc[768:896, :] * node_scale
    eib[...] = sums_sc[896:897, :] * edge_scale
    eob[...] = sums_sc[897:898, :] * edge_scale
    nib[...] = sums_sc[898:899, :] * node_scale
    nob[...] = sums_sc[899:900, :] * node_scale


def call(kernel, out_shapes, specs, scratch, args, flops, moved):
    return pl.pallas_call(
        kernel,
        out_shape=[jax.ShapeDtypeStruct(shape, dtype) for shape, dtype in out_shapes],
        in_specs=specs,
        out_specs=[VMEM] * len(out_shapes),
        scratch_shapes=scratch,
        compiler_params=pltpu.CompilerParams(vmem_limit_bytes=40 * 1024 * 1024),
        cost_estimate=pl.CostEstimate(flops=flops, bytes_accessed=moved, transcendentals=0),
    )(*args)


def in_hbm(*values):
    return tuple(pltpu.with_memory_space_constraint(value, pltpu.HBM) for value in values)


def exchanged(messages):
    def near(device):
        return device ^ 1

    def next_chip(device):
        return device + 1 if device % 2 else device - 1

    count = lax.axis_size(AXES)
    quarter = count // 4

    def far_up(device):
        return device + quarter if (device // quarter) % 2 == 0 else device - quarter

    def far_down(device):
        return device - quarter if (device // quarter) % 2 == 0 else device + quarter

    def swapped(message, swap):
        return lax.ppermute(message, AXES, [(s, swap(s) % count) for s in range(count)])

    swaps = (next_chip, far_up, far_down, near)
    return [swapped(message, swap) for message, swap in zip(messages, swaps)]


def swapped_with(value, axis, partner):
    return lax.ppermute(value, axis, [(s, partner(s)) for s in range(lax.axis_size(axis))])


def summed_along_y(mine, theirs):
    half = mine + swapped_with(theirs, "c", lambda s: 1 - s)
    blocks = [half[k * QUARTER : (k + 1) * QUARTER] for k in range(4)]
    one = swapped_with(blocks[1], "y", lambda s: s ^ 1)
    three = swapped_with(blocks[3], "y", lambda s: s ^ 3)
    two = swapped_with(blocks[2], "y", lambda s: s ^ 2)
    one, three, two = lax.optimization_barrier((one, three, two))
    return (blocks[0] + one) + (two + three)


def summed_along_z(total):
    one = swapped_with(total, "z", lambda s: s ^ 1)
    three = swapped_with(total, "z", lambda s: s ^ 3)
    two = swapped_with(total, "z", lambda s: s ^ 2)
    one, three, two = lax.optimization_barrier((one, three, two))
    return (total + one) + (two + three)


def shared(total):
    one = swapped_with(total, "y", lambda s: s ^ 1)
    three = swapped_with(total, "y", lambda s: s ^ 3)
    two = swapped_with(total, "y", lambda s: s ^ 2)
    one, three, two = lax.optimization_barrier((one, three, two))
    own = jnp.concatenate([total, one, two, three], axis=0)
    return own, swapped_with(own, "c", lambda s: 1 - s)


def body(
    node_features,
    edge_features,
    node_cotangent,
    edge_cotangent,
    edge_in_weight,
    edge_in_bias,
    edge_out_weight,
    edge_out_bias,
    node_in_weight,
    node_in_bias,
    node_out_weight,
    edge_ends,
    live_elements,
    shared_nodes,
    shared_counts,
    multiplicity,
):
    nodes, width = node_features.shape
    edges = edge_features.shape[0]
    devices = lax.axis_size(AXES)
    element_edges = edge_ends.shape[1]
    lists = shared_nodes.reshape(shared_nodes.shape[1:])
    copies = multiplicity.reshape(nodes // LANES, LANES)
    message = ((LANES, width), F32)
    node_f32 = ((nodes, width), F32)
    node_bf16 = ((nodes, width), BF16)
    both_f32 = ((element_edges, 2 * LANES), F32)
    both_bf16 = ((element_edges, 2 * LANES), BF16)
    edge_bf16 = ((edges, width), BF16)
    rows_height = padded(element_edges)
    ends_scratch = pltpu.VMEM((8, rows_height), jnp.int32)
    listed = 4 * LANES

    forward_args = in_hbm(
        shared_counts,
        edge_ends,
        lists,
        node_features,
        edge_features,
        edge_in_weight,
        edge_in_bias.reshape(1, -1),
        edge_out_weight,
        edge_out_bias.reshape(1, -1),
    )
    aggregate, *messages, edge_hidden, edge_slope, table, spread_target, pick = call(
        forward_kernel,
        [node_f32]
        + [message] * 4
        + [
            both_bf16,
            both_f32,
            ((element_edges, NPE), BF16),
            ((NPE, rows_height), BF16),
            ((listed, nodes), BF16),
        ],
        [HBM] * 9,
        [pltpu.SMEM(shared_counts.shape, jnp.int32)]
        + [pltpu.VMEM(arg.shape, arg.dtype) for arg in forward_args[1:]]
        + [
            pltpu.SemaphoreType.DMA((9,)),
            ends_scratch,
            pltpu.VMEM((rows_height, 2 * LANES), BF16),
            pltpu.VMEM((element_edges, NPE), BF16),
        ],
        forward_args,
        2_000_000_000,
        4_000_000,
    )
    arrived = exchanged(messages)
    spread_source, arrive, linear_part, hidden_back, node_cot, node_shares = call(
        prepare_kernel,
        [
            ((NPE, rows_height), BF16),
            ((nodes, listed), BF16),
            node_f32,
            node_f32,
            node_bf16,
            node_f32,
        ],
        [SMEM, SMEM] + [VMEM] * 8,
        [ends_scratch],
        (
            shared_counts,
            live_elements,
            edge_ends,
            lists,
            copies,
            node_features,
            node_cotangent,
            node_in_weight,
            node_in_bias.reshape(1, -1),
            node_out_weight,
        ),
        1_000_000_000,
        4_000_000,
    )
    consistent_back, *messages, consistent, node_hidden, node_back = call(
        node_kernel,
        [node_f32] + [message] * 4 + [node_bf16] * 3,
        [VMEM] * 11,
        [],
        (
            aggregate,
            *arrived,
            arrive,
            pick,
            linear_part,
            hidden_back,
            node_shares,
            node_in_weight,
        ),
        600_000_000,
        4_000_000,
    )
    arrived = exchanged(messages)
    node_part, node_terms, given, edges_across, nodes_across, sums_across, out_part, out_across = call(
        side_kernel,
        [
            node_f32,
            ((448, width), F32),
            both_bf16,
            ((2 * LANES, rows_height), BF16),
            ((width, nodes), BF16),
            ((2 * width, nodes), BF16),
            message,
            ((2 * LANES, 2 * LANES), BF16),
        ],
        [SMEM] + [VMEM] * 11,
        [],
        (
            live_elements,
            node_features,
            consistent,
            node_hidden,
            node_back,
            node_cot,
            node_in_weight,
            edge_features,
            edge_cotangent,
            edge_hidden,
            spread_target,
            edge_out_weight,
        ),
        1_000_000_000,
        4_000_000,
    )
    half_terms = ((4 * QUARTER, width), F32)
    edge_cot, edge_back, edge_sums, mine, theirs = call(
        backward_kernel,
        [
            both_f32,
            ((rows_height, 2 * LANES), BF16),
            ((nodes, 2 * LANES), F32),
            half_terms,
            half_terms,
        ],
        [VMEM] * 17,
        [pltpu.VMEM((8 * QUARTER, LANES), F32)],
        (
            consistent_back,
            *arrived,
            arrive,
            table,
            spread_source,
            spread_target,
            given,
            edge_slope,
            edges_across,
            nodes_across,
            sums_across,
            out_part,
            node_terms,
            out_across,
        ),
        2_000_000_000,
        6_000_000,
    )
    total = summed_along_y(mine, theirs)
    total = summed_along_z(total)
    total, edge_cot = lax.optimization_barrier((total, edge_cot))
    far = swapped_with(total, "z", lambda s: 7 - s)
    node_result, edge_result = call(
        results_kernel,
        [node_bf16, edge_bf16],
        [VMEM] * 5,
        [],
        (edge_cot, edge_back, edge_sums, node_part, edge_in_weight),
        2_000_000_000,
        6_000_000,
    )
    total, far, node_result = lax.optimization_barrier((total, far, node_result))
    own, other = shared(total + far)
    edge_scale = 1.0 / math.sqrt(edges * devices)
    node_scale = 1.0 / math.sqrt(nodes * devices)

    def finish(*refs):
        finish_kernel(edge_scale, node_scale, *refs)

    ei, eib, eo, eob, ni, nib, no, nob = call(
        finish,
        [
            ((384, width), F32),
            ((1, width), F32),
            ((128, width), F32),
            ((1, width), F32),
            ((256, width), F32),
            ((1, width), F32),
            ((128, width), F32),
            ((1, width), F32),
        ],
        [VMEM] * 2,
        [pltpu.VMEM((8 * QUARTER, LANES), F32)],
        (own, other),
        1_000_000,
        1_000_000,
    )
    return (
        node_result,
        edge_result,
        ei,
        eib.reshape(-1),
        eo,
        eob.reshape(-1),
        ni,
        nib.reshape(-1),
        no,
        nob.reshape(-1),
    )


def solution(mesh):
    grid = mesh.devices.reshape(8, 4, 2, 4)
    mesh = Mesh(grid, ("z", "y", "c", "rep"))
    rows = ("rep", "z", "y", "c")
    in_specs = (
        P(rows, None),
        P(rows, None),
        P(rows, None),
        P(rows, None),
        P(),
        P(),
        P(),
        P(),
        P(),
        P(),
        P(),
        P(),
        P(rows),
        P(rows, None, None),
        P(rows, None),
        P(rows),
    )
    out_specs = (
        P(rows, None),
        P(rows, None),
        P("rep", None),
        P("rep"),
        P("rep", None),
        P("rep"),
        P("rep", None),
        P("rep"),
        P("rep", None),
        P("rep"),
    )
    return jax.shard_map(body, mesh=mesh, in_specs=in_specs, out_specs=out_specs, check_vma=False)
```
